32 devices in a mesh: groups: 2 (over y), seq: 4 (over z), batch: 2 (over x), head: 2 (over core).
Axes of the slice: x: 2, y: 2, z: 4, core: 2. Of those that a mesh axis runs over, the one named last changes fastest.
Arguments:
- query_in: bfloat16 [4, 2048, 1024], P(('groups', 'batch'), 'seq', 'head'), parts along dimension 0, may hold values from -1.5 to 1.5
- key_in: bfloat16 [4, 2048, 1024], P(('groups', 'batch'), 'seq', 'head'), parts along dimension 0, may hold values from -1.5 to 1.5
- value_in: bfloat16 [4, 2048, 1024], P(('groups', 'batch'), 'seq', 'head'), parts along dimension 0, may hold values from -6 to 6
- level_mask: int32 [4, 2048, 16], P(('groups', 'batch'), 'seq'), parts along dimension 0, may hold values 0 or 1
- out_weight: bfloat16 [1024, 2048], P('head'), may hold values from -0.1875 to 0.1875
- grad_out: bfloat16 [4, 2048, 2048], P(('groups', 'batch'), 'seq', 'head'), parts along dimension 0, may hold values from -0.8984375 to 0.8984375
Outputs:
- layer_out: bfloat16 [4, 2048, 2048], P(('groups', 'batch'), 'seq', 'head'), parts along dimension 0
- grad_query: bfloat16 [4, 2048, 1024], P(('groups', 'batch'), 'seq', 'head'), parts along dimension 0
- grad_key: bfloat16 [4, 2048, 1024], P(('groups', 'batch'), 'seq', 'head'), parts along dimension 0
- grad_value: bfloat16 [4, 2048, 1024], P(('groups', 'batch'), 'seq', 'head'), parts along dimension 0
The draws below stay inside these ranges and needn't reach their ends.
There are 2 independent parts, one for each index of `groups`. The reference program is written for one: setup_inputs(seed, part) draws one part's arguments, and reference() takes and returns one part's arrays. A program takes and returns all parts, laid end to end along the dimension named above; an argument that names none is the same for every part. Nothing has to cross between parts.
All inputs are finite; a program needn't handle non-finite values. No bound on the sum of `level_mask` on one device may be relied on, other than what follows from the above.
Results may differ from the reference program's by a relative error of at most 0.0091.
Values may be sent and summed in bfloat16 or wider, within the bound.
No kernel may reach another device: no remote copies, remote signals or barrier semaphores. Data moves between devices by JAX's collectives and lax.ppermute only.
A program may use at most 64 MiB of HBM per device.

```python
import jax
import jax.numpy as jnp
import numpy as np
from jax import lax

D = 2048
H = 8
HEAD_DIM = 128
LEVEL_SLOTS = 16
TOK_DEV = 512
BATCH = 2
TOKENS = 2048
N_SEQ = 4


def with_ends(values, stream_key, low, largest):
    spot = [jax.random.randint(jax.random.fold_in(stream_key, axis), (), 0, length) for axis, length in enumerate(values.shape)]
    main_axis = values.shape.index(max(values.shape))
    neighbour = spot[:main_axis] + [(spot[main_axis] + 1) % values.shape[main_axis]] + spot[main_axis + 1:]
    return values.at[tuple(spot)].set(low).at[tuple(neighbour)].set(largest)


def shard_levels(own_key, shape, cuts, low, top_value):
    level, own = 1.0, jax.random.fold_in(own_key, 6)
    for axis_at, blocks in cuts:
        draws = jnp.exp(jax.random.uniform(jax.random.fold_in(own, axis_at), (blocks,), jnp.float32, low / len(cuts), top_value / len(cuts)))
        level = level * jnp.repeat(draws, shape[axis_at] // blocks).reshape([-1 if axis == axis_at else 1 for axis in range(len(shape))])
    return level


def noise(own_key, shape, width, most, cuts=(), kind=jnp.bfloat16):
    values = width * jax.random.normal(own_key, shape, jnp.float32)
    if cuts:
        values = values * shard_levels(own_key, shape, cuts, -0.22, 0.18)
    return jnp.clip(values, -most, most).astype(kind)


def setup_inputs(seed: int = 0, part: int = 0) -> dict:
    key_of = jax.random.split(jax.random.key(seed), 7)
    part_splits = jax.random.split(jax.random.fold_in(key_of[6], part), 7)
    return {
        "query_in": noise(part_splits[0], (BATCH, TOKENS, H * HEAD_DIM), 0.25, 1.5, ((0, 2), (1, 4), (2, 2))),
        "key_in": noise(part_splits[1], (BATCH, TOKENS, H * HEAD_DIM), 0.25, 1.5, ((0, 2), (1, 4), (2, 2))),
        "value_in": noise(part_splits[2], (BATCH, TOKENS, H * HEAD_DIM), 1.0, 6.0, ((0, 2), (1, 4), (2, 2))),
        "level_mask": with_ends((jax.random.randint(part_splits[3], (BATCH, TOKENS, LEVEL_SLOTS), 0, 4) < 3).astype(jnp.int32), jax.random.fold_in(part_splits[3], 1), 0, 1),
        "out_weight": noise(key_of[4], (H * HEAD_DIM, D), (H * HEAD_DIM) ** -0.5, 0.1875, ((0, 2),)),
        "grad_out": noise(part_splits[5], (BATCH, TOKENS, D), 0.15, 0.8984375, ((0, 2), (1, 4), (2, 2))),
    }


level_scale = np.array([1.0] + [2.0 ** (-(tier - 1) / 2.0) for tier in range(1, 16)], dtype=np.float32)
HIGHEST = lax.Precision.HIGHEST


def top_bit(values):
    result = jnp.zeros_like(values)
    for power in range(1, 24):
        result = result + (values >= (1 << power)).astype(jnp.int32)
    return result


def block_levels(count):
    rows = jnp.arange(count, dtype=jnp.int32)
    later = rows[:, None]
    earlier = rows[None, :]
    spread = jnp.bitwise_xor(later, earlier)
    depth_map = jnp.where(spread == 0, 0, 1 + top_bit(jnp.maximum(spread, 1)))
    inside = earlier <= later
    return jnp.stack([((depth_map == tier) & inside).astype(jnp.float32) for tier in range(count.bit_length())])


def block_routes(count, span):
    rows = jnp.arange(count, dtype=jnp.int32)
    later = rows[:, None]
    earlier = rows[None, :]
    tier_of = top_bit(jnp.maximum(jnp.bitwise_xor(later, earlier), 1))
    return jnp.stack([((earlier < later) & (tier_of == tier)).astype(jnp.float32) for tier in range(span)])


def to_low(values):
    return lax.optimization_barrier(values.astype(jnp.bfloat16)).astype(jnp.float32)


def one_sequence(inputs, out_weight):
    query_seq, key_seq, value_seq, mask_seq, grad_seq = inputs
    shape_blocks = (N_SEQ, TOK_DEV, H, HEAD_DIM)
    query_rows = query_seq.reshape(shape_blocks).astype(jnp.float32)
    key_rows = key_seq.reshape(shape_blocks).astype(jnp.float32)
    value_rows = value_seq.reshape(shape_blocks).astype(jnp.float32)
    weights = mask_seq.astype(jnp.float32).reshape(N_SEQ, TOK_DEV, LEVEL_SLOTS) * jnp.asarray(level_scale, dtype=jnp.float32)
    tiers = TOK_DEV.bit_length()
    span = N_SEQ.bit_length() - 1
    intra_map = block_levels(TOK_DEV)
    blend = jnp.einsum('lts,ntl->nts', intra_map, weights[:, :, :tiers], precision=HIGHEST)
    scores = jnp.einsum('nthd,nshd->nhts', query_rows, key_rows, precision=HIGHEST)
    probs = (scores * blend[:, None]).astype(jnp.bfloat16).astype(jnp.float32)
    local_out = jnp.einsum('nhts,nshd->nthd', probs, value_rows, precision=HIGHEST)
    block_state = jnp.einsum('nthd,nthe->nhde', key_rows, value_rows, precision=HIGHEST)
    routes = block_routes(N_SEQ, span)
    states = jnp.einsum('jbc,chde->jbhde', routes, block_state, precision=HIGHEST)
    states_low = to_low(states)
    tier_weight = weights[:, :, tiers:tiers + span]
    weighted_query = to_low(jnp.transpose(tier_weight, (2, 0, 1))[:, :, :, None, None] * query_rows[None])
    far_out = jnp.einsum('jnthd,jnhde->nthe', weighted_query, states_low, precision=HIGHEST)
    mixed = (local_out + far_out).astype(jnp.bfloat16).reshape(TOKENS, H * HEAD_DIM)
    layer = jnp.dot(mixed, out_weight, preferred_element_type=jnp.float32).astype(jnp.bfloat16)
    grad_mixed = jnp.dot(grad_seq, out_weight.T, preferred_element_type=jnp.float32).astype(jnp.bfloat16)
    grad_rows = grad_mixed.reshape(shape_blocks).astype(jnp.float32)
    dprob = jnp.einsum('nthe,nshe->nhts', grad_rows, value_rows, precision=HIGHEST)
    dscore = (dprob * blend[:, None]).astype(jnp.bfloat16).astype(jnp.float32)
    query_local = jnp.einsum('nhts,nshd->nthd', dscore, key_rows, precision=HIGHEST)
    key_local = jnp.einsum('nhts,nthd->nshd', dscore, query_rows, precision=HIGHEST)
    value_local = jnp.einsum('nhts,nthe->nshe', probs, grad_rows, precision=HIGHEST)
    query_far = jnp.einsum('ntj,nthe,jnhde->nthd', tier_weight, grad_rows, states_low, precision=HIGHEST)
    reach = jnp.einsum('jnthd,nthe->jnhde', weighted_query, grad_rows, precision=HIGHEST)
    back = jnp.einsum('jbc,jbhde->chde', routes, reach, precision=HIGHEST)
    back_low = to_low(back)
    key_far = jnp.einsum('chde,cshe->cshd', back_low, value_rows, precision=HIGHEST)
    value_far = jnp.einsum('chde,cshd->cshe', back_low, key_rows, precision=HIGHEST)
    flat = (TOKENS, H * HEAD_DIM)
    grad_query = (query_local + query_far).astype(jnp.bfloat16).reshape(flat)
    grad_key = (key_local + key_far).astype(jnp.bfloat16).reshape(flat)
    grad_value = (value_local + value_far).astype(jnp.bfloat16).reshape(flat)
    return layer, grad_query, grad_key, grad_value


def reference(query_in, key_in, value_in, level_mask, out_weight, grad_out):
    def apply_one(inputs):
        return one_sequence(inputs, out_weight)
    layer_out, grad_query, grad_key, grad_value = lax.map(apply_one, (query_in, key_in, value_in, level_mask, grad_out))
    return (layer_out, grad_query, grad_key, grad_value)
```

```python
import functools

import jax
import jax.numpy as jnp
from jax import lax
from jax.experimental import pallas as pl
from jax.experimental.pallas import tpu as pltpu
from jax.sharding import PartitionSpec as P

HEAD_DIM = 128
TILE = 256
F32 = jnp.float32
BF16 = jnp.bfloat16
VMEM = pl.BlockSpec(memory_space=pltpu.VMEM)
SMEM = pl.BlockSpec(memory_space=pltpu.SMEM)


def level_scale(level):
    return 1.0 if level == 0 else 2.0 ** (-(level - 1) / 2.0)


def dot(a, b):
    return lax.dot_general(a, b, (((1,), (0,)), ((), ())), preferred_element_type=F32)


def dot_nt(a, b):
    return lax.dot_general(a, b, (((1,), (1,)), ((), ())), preferred_element_type=F32)


def dot_tn(a, b):
    return lax.dot_general(a, b, (((0,), (0,)), ((), ())), preferred_element_type=F32)


def tier(mask, level):
    return mask[:, level : level + 1].astype(F32) * jnp.float32(level_scale(level))


def call(kernel, name, out_shape, in_specs, flops, *args):
    moved = sum(a.size * a.dtype.itemsize for a in args)
    moved += sum(o.size * o.dtype.itemsize for o in out_shape)
    return pl.pallas_call(
        kernel,
        name=name,
        out_shape=out_shape,
        in_specs=in_specs,
        out_specs=[VMEM] * len(out_shape),
        compiler_params=pltpu.CompilerParams(vmem_limit_bytes=16 << 20),
        cost_estimate=pl.CostEstimate(flops=flops, bytes_accessed=moved, transcendentals=0),
    )(*args)


def head_slices(width):
    return [slice(i * HEAD_DIM, (i + 1) * HEAD_DIM) for i in range(width // HEAD_DIM)]


def state_kernel(key_ref, value_ref, state_ref):
    for col in head_slices(key_ref.shape[1]):
        state_ref[col, :] = dot_tn(key_ref[:, col], value_ref[:, col]).astype(BF16)


def own_kernel(place_ref, grad_ref, weight_ref, part_ref, quarter_ref):
    half = grad_ref.shape[1]
    mine = pl.multiple_of(place_ref[0] * half, half)
    other = pl.multiple_of((1 - place_ref[0]) * half, half)
    part_ref[...] = dot_nt(grad_ref[...], weight_ref[:, pl.ds(mine, half)])
    quarter_ref[...] = weight_ref[:, pl.ds(other, half)]


def reach_kernel(tiers, place_ref, grad_ref, weight_ref, part_ref, query_ref, mask_ref, *outs):
    grad_mixed_ref, weighted_ref, reach_refs = outs[0], outs[1], outs[2:]
    span = len(reach_refs)
    half = grad_ref.shape[1]
    other = pl.multiple_of((1 - place_ref[0]) * half, half)
    mask = mask_ref[...]
    weight = [tier(mask, tiers + j) for j in range(span)]
    for i, col in enumerate(head_slices(query_ref.shape[1])):
        rows = weight_ref[col, pl.ds(other, half)]
        grad = (part_ref[:, col] + dot_nt(grad_ref[...], rows)).astype(BF16)
        grad_mixed_ref[:, col] = grad
        query = query_ref[:, col].astype(F32)
        weighted = [(w * query).astype(BF16) for w in weight]
        for j in range(span):
            at = (i * span + j) * HEAD_DIM
            weighted_ref[:, at : at + HEAD_DIM] = weighted[j]
            reach_refs[j][col, :] = dot_tn(weighted[j], grad).astype(BF16)


def tile_blend(mask, tile):
    rows = lax.broadcasted_iota(jnp.int32, (tile, tile), 0)
    cols = lax.broadcasted_iota(jnp.int32, (tile, tile), 1)
    spread = rows ^ cols
    blend = jnp.where(spread == 0, tier(mask, 0), 0.0)
    for level in range(1, tile.bit_length()):
        here = ((spread >> (level - 1)) == 1) & (cols < rows)
        blend = jnp.where(here, tier(mask, level), blend)
    return blend


def local_kernel(query_ref, key_ref, value_ref, grad_ref, mask_ref, mixed_ref, dq_ref, dk_ref, dv_ref):
    length, width = query_ref.shape
    tile = min(TILE, length)
    count = length // tile
    inner = tile.bit_length()
    bits = count.bit_length() - 1
    span = [slice(i * tile, (i + 1) * tile) for i in range(count)]
    mask = mask_ref[...]
    blends = [tile_blend(mask[rows], tile) for rows in span]
    for col in head_slices(width):
        query = [query_ref[rows, col] for rows in span]
        key = [key_ref[rows, col] for rows in span]
        value = [value_ref[rows, col] for rows in span]
        grad = [grad_ref[rows, col] for rows in span]
        state = [dot_tn(key[i], value[i]) for i in range(count)] if count > 1 else []
        back = [None] * count
        for i in range(count):
            probs = (blends[i] * dot_nt(query[i], key[i])).astype(BF16)
            dscore = (blends[i] * dot_nt(grad[i], value[i])).astype(BF16)
            mixed = dot(probs, value[i])
            dq = dot(dscore, key[i])
            for b in range(bits):
                if not i >> b & 1:
                    continue
                first = ((i >> b) ^ 1) << b
                total = functools.reduce(jnp.add, state[first : first + (1 << b)]).astype(BF16)
                weight = tier(mask[span[i]], inner + b)
                weighted = (weight * query[i].astype(F32)).astype(BF16)
                mixed = mixed + dot(weighted, total)
                dq = dq + weight * dot_nt(grad[i], total)
                reach = dot_tn(weighted, grad[i])
                for m in range(first, first + (1 << b)):
                    back[m] = reach if back[m] is None else back[m] + reach
            mixed_ref[span[i], col] = mixed
            dq_ref[span[i], col] = dq
            dk_ref[span[i], col] = dot_tn(dscore, query[i])
            dv_ref[span[i], col] = dot_tn(probs, grad[i])
        for i in range(count):
            if back[i] is not None:
                low = back[i].astype(BF16)
                dk_ref[span[i], col] += dot_nt(value[i], low)
                dv_ref[span[i], col] += dot(key[i], low)


def mixed_kernel(flag_ref, mixed_ref, weighted_ref, *refs):
    state_refs, out_ref = refs[:-1], refs[-1]
    span = len(state_refs)
    for i, col in enumerate(head_slices(mixed_ref.shape[1])):
        states = [(state_refs[j][col, :].astype(F32) * flag_ref[j]).astype(BF16) for j in range(span)]
        at = i * span * HEAD_DIM
        far = dot(weighted_ref[:, at : at + span * HEAD_DIM], jnp.concatenate(states, axis=0))
        out_ref[:, col] = (mixed_ref[:, col] + far).astype(BF16)


def query_kernel(tiers, flag_ref, place_ref, dq_ref, grad_ref, mask_ref, mixed_ref, weight_ref, *refs):
    state_refs, out_ref, part_ref = refs[:-2], refs[-2], refs[-1]
    half = part_ref.shape[1]
    mine = pl.multiple_of(place_ref[0] * half, half)
    part_ref[...] = dot(mixed_ref[...], weight_ref[:, pl.ds(mine, half)])
    mask = mask_ref[...]
    weight = [tier(mask, tiers + j) * flag_ref[j] for j in range(len(state_refs))]
    for col in head_slices(dq_ref.shape[1]):
        total = dq_ref[:, col]
        for j, ref in enumerate(state_refs):
            total = total + weight[j] * dot_nt(grad_ref[:, col], ref[col, :])
        out_ref[:, col] = total.astype(BF16)


def layer_kernel(part_ref, mixed_ref, quarter_ref, out_ref):
    out_ref[...] = (part_ref[...] + dot(mixed_ref[...], quarter_ref[...])).astype(BF16)


def back_kernel(dk_ref, dv_ref, key_ref, value_ref, *refs):
    back_refs, dk_out, dv_out = refs[:-2], refs[-2], refs[-1]
    for col in head_slices(key_ref.shape[1]):
        back = functools.reduce(jnp.add, [ref[col, :].astype(F32) for ref in back_refs]).astype(BF16)
        dk_out[:, col] = (dk_ref[:, col] + dot_nt(value_ref[:, col], back)).astype(BF16)
        dv_out[:, col] = (dv_ref[:, col] + dot(key_ref[:, col], back)).astype(BF16)


def pairs(count, stride, up=True, down=True):
    route = []
    for low in range(count):
        high = low ^ stride
        if low < high < count:
            route += [(low, high)] * up + [(high, low)] * down
    return route


def add_low(a, b):
    return (a.astype(F32) + b.astype(F32)).astype(BF16)


def on_device(query_in, key_in, value_in, level_mask, out_weight, grad_out):
    blocks = lax.axis_size("seq")
    if query_in.shape[0] != 1 or lax.axis_size("head") != 2 or blocks < 2:
        raise ValueError("unsupported split")
    query, key, value, mask, grad = (x[0] for x in (query_in, key_in, value_in, level_mask, grad_out))
    length, width = query.shape
    half = grad.shape[1]
    tiers = length.bit_length()
    span = blocks.bit_length() - 1
    position = lax.axis_index("seq")
    place = lax.axis_index("head").astype(jnp.int32)[None]
    flags = ((position >> jnp.arange(span, dtype=jnp.int32)) & 1).astype(F32)
    swap = [(0, 1), (1, 0)]
    shape = jax.ShapeDtypeStruct
    matrix = shape((width, HEAD_DIM), BF16)
    low = shape((length, width), BF16)
    high = shape((length, width), F32)
    unit = 2 * length * width * HEAD_DIM

    with jax.named_scope("grad_swap"):
        grad_other = lax.ppermute(grad, "head", swap)
    (state,) = call(state_kernel, "state", [matrix], [VMEM] * 2, unit, key, value)
    states, total = [], state
    part, quarter = call(
        own_kernel,
        "own",
        [high, shape((width, half), BF16)],
        [SMEM, VMEM, VMEM],
        2 * length * width * half,
        place,
        grad,
        out_weight,
    )
    with jax.named_scope("weight_swap"):
        quarter = lax.ppermute(quarter, "head", swap)
    for j in range(span):
        with jax.named_scope(f"state_step{j}"):
            got = lax.ppermute(total, "seq", pairs(blocks, 1 << j, down=j < span - 1))
        states.append(got)
        if j < span - 1:
            total = add_low(total, got)

    grad_mixed, weighted, *pending = call(
        functools.partial(reach_kernel, tiers),
        "reach",
        [low, shape((length, span * width), BF16)] + [matrix] * span,
        [SMEM] + [VMEM] * 5,
        2 * length * width * half + span * unit,
        place,
        grad_other,
        out_weight,
        part,
        query,
        mask,
    )
    backs = []
    for j in range(span):
        with jax.named_scope(f"reach_step{j}"):
            later = [lax.ppermute(x, "seq", pairs(blocks, 1 << j)) for x in pending[1:]]
            backs.append(lax.ppermute(pending[0], "seq", pairs(blocks, 1 << j, up=False)))
        pending = [add_low(a, b) for a, b in zip(pending[1:], later)]

    mixed, dq, dk, dv = call(
        local_kernel,
        "local",
        [high] * 4,
        [VMEM] * 5,
        6 * 2 * unit,
        query,
        key,
        value,
        grad_mixed,
        mask,
    )
    (mixed,) = call(
        mixed_kernel, "mixed", [low], [SMEM] + [VMEM] * (2 + span), span * unit, flags, mixed, weighted, *states
    )
    with jax.named_scope("mixed_swap"):
        mixed_other = lax.ppermute(mixed, "head", swap)
    grad_query, part = call(
        functools.partial(query_kernel, tiers),
        "query",
        [low, shape((length, half), F32)],
        [SMEM] * 2 + [VMEM] * (5 + span),
        2 * length * width * half + span * unit,
        flags,
        place,
        dq,
        grad_mixed,
        mask,
        mixed,
        out_weight,
        *states,
    )
    (layer_out,) = call(
        layer_kernel,
        "layer",
        [shape((length, half), BF16)],
        [VMEM] * 3,
        2 * length * width * half,
        part,
        mixed_other,
        quarter,
    )
    grad_key, grad_value = call(
        back_kernel, "back", [low] * 2, [VMEM] * (4 + span), 2 * unit, dk, dv, key, value, *backs
    )
    return tuple(x[None] for x in (layer_out, grad_query, grad_key, grad_value))


def solution(mesh):
    rows = P(("groups", "batch"), "seq", "head")
    return jax.shard_map(
        on_device,
        mesh=mesh,
        in_specs=(rows, rows, rows, P(("groups", "batch"), "seq", None), P("head", None), rows),
        out_specs=(rows,) * 4,
        check_vma=False,
    )
```

```python
import functools

import jax
import jax.numpy as jnp
from jax import lax
from jax.experimental import pallas as pl
from jax.experimental.pallas import tpu as pltpu
from jax.sharding import PartitionSpec as P

HEAD_DIM = 128
TILE = 256
DIRECT = 4
F32 = jnp.float32
BF16 = jnp.bfloat16
VMEM = pl.BlockSpec(memory_space=pltpu.VMEM)
SMEM = pl.BlockSpec(memory_space=pltpu.SMEM)
HBM = pl.BlockSpec(memory_space=pltpu.HBM)


def level_scale(level):
    return 1.0 if level == 0 else 2.0 ** (-(level - 1) / 2.0)


def dot(a, b):
    return lax.dot_general(a, b, (((1,), (0,)), ((), ())), preferred_element_type=F32)


def dot_nt(a, b):
    return lax.dot_general(a, b, (((1,), (1,)), ((), ())), preferred_element_type=F32)


def dot_tn(a, b):
    return lax.dot_general(a, b, (((0,), (0,)), ((), ())), preferred_element_type=F32)


def call(kernel, outs, in_specs, flops, args, out_specs=None, scratch=(), limit=16):
    moved = sum(a.size * a.dtype.itemsize for a in args)
    moved += sum(o.size * o.dtype.itemsize for o in outs)
    return pl.pallas_call(
        kernel,
        out_shape=outs,
        in_specs=in_specs,
        out_specs=out_specs or [VMEM] * len(outs),
        scratch_shapes=list(scratch),
        compiler_params=pltpu.CompilerParams(vmem_limit_bytes=limit << 20),
        cost_estimate=pl.CostEstimate(flops=flops, bytes_accessed=moved, transcendentals=0),
    )(*args)


def head_slices(width):
    return [slice(i * HEAD_DIM, (i + 1) * HEAD_DIM) for i in range(width // HEAD_DIM)]


def upper(spot_ref, bit):
    return (spot_ref[0] >> bit) & 1


def column(ref, index):
    half = ref.shape[1] // 2
    return ref.at[:, pl.ds(pl.multiple_of(index * half, half), half)]


def prep_kernel(tiers, span, *refs):
    place_ref, mask_ref, key_hbm, value_hbm, grad_hbm, weight_hbm, query_hbm = refs[:7]
    state_ref, part_ref, weighted_ref, tier_ref = refs[7:11]
    key, value, grad, weight, query, sems = refs[11:]
    sources = [key_hbm, value_hbm, column(weight_hbm, place_ref[0]), grad_hbm, query_hbm]
    copies = [
        pltpu.make_async_copy(src, dst, sems.at[n])
        for n, (src, dst) in enumerate(zip(sources, [key, value, weight, grad, query]))
    ]
    for copy in copies:
        copy.start()
    slots = mask_ref.shape[0]
    mask = mask_ref[...].astype(F32)
    rows = [mask[l : l + 1] * jnp.float32(level_scale(l)) for l in range(slots)]
    tier = jnp.transpose(jnp.concatenate(rows, axis=0))
    tier_ref[...] = tier
    copies[0].wait()
    copies[1].wait()
    cols = head_slices(key.shape[1])
    for col in cols:
        state_ref[col, :] = dot_tn(key[:, col], value[:, col]).astype(BF16)
    copies[2].wait()
    copies[3].wait()
    part_ref[...] = dot_nt(grad[...], weight[...])
    copies[4].wait()
    for j in range(span):
        scale = jnp.broadcast_to(tier[:, tiers + j : tiers + j + 1], (tier.shape[0], HEAD_DIM))
        for i, col in enumerate(cols):
            at = (i * span + j) * HEAD_DIM
            weighted_ref[:, at : at + HEAD_DIM] = (scale * query[:, col].astype(F32)).astype(BF16)


def reach_kernel(span, direct, place_ref, spot_ref, grad_ref, weight_ref, part_ref, weighted_ref, state_ref, *outs):
    grad_mixed_ref, send_refs = outs[0], outs[1:]
    other = column(weight_ref, 1 - place_ref[0])
    grad_mixed = (part_ref[...] + dot_nt(grad_ref[...], other[...])).astype(BF16)
    grad_mixed_ref[...] = grad_mixed
    step = span * HEAD_DIM
    for i, col in enumerate(head_slices(grad_mixed.shape[1])):
        reach = dot_tn(grad_mixed[:, col], weighted_ref[:, i * step : (i + 1) * step])
        state = state_ref[col, :].astype(F32)
        for j in range(span):
            send = reach[:, j * HEAD_DIM : (j + 1) * HEAD_DIM]
            if direct:
                send = jnp.where(upper(spot_ref, j) > 0, send, state)
            send_refs[j][col, :] = send.astype(BF16)


def tile_blend(tier, tile):
    rows = lax.broadcasted_iota(jnp.int32, (tile, tile), 0)
    cols = lax.broadcasted_iota(jnp.int32, (tile, tile), 1)
    spread = rows ^ cols
    blend = jnp.where(spread == 0, tier[:, 0:1], 0.0)
    for level in range(1, tile.bit_length()):
        here = ((spread >> (level - 1)) == 1) & (cols < rows)
        blend = jnp.where(here, tier[:, level : level + 1], blend)
    return blend


def local_kernel(query_ref, key_ref, value_ref, grad_ref, tier_ref, mixed_ref, dq_ref, dk_ref, dv_ref):
    length, width = query_ref.shape
    tile = min(TILE, length)
    count = length // tile
    inner = tile.bit_length()
    bits = count.bit_length() - 1
    span = [slice(i * tile, (i + 1) * tile) for i in range(count)]
    tiers = [tier_ref[rows, :] for rows in span]
    blends = [tile_blend(tier, tile) for tier in tiers]
    for col in head_slices(width):
        query = [query_ref[rows, col] for rows in span]
        key = [key_ref[rows, col] for rows in span]
        value = [value_ref[rows, col] for rows in span]
        grad = [grad_ref[rows, col] for rows in span]
        state = [dot_tn(key[i], value[i]) for i in range(count)] if count > 1 else []
        back = [None] * count
        for i in range(count):
            probs = (blends[i] * dot_nt(query[i], key[i])).astype(BF16)
            dscore = (blends[i] * dot_nt(grad[i], value[i])).astype(BF16)
            mixed = dot(probs, value[i])
            dq = dot(dscore, key[i])
            for b in range(bits):
                if not i >> b & 1:
                    continue
                first = ((i >> b) ^ 1) << b
                total = functools.reduce(jnp.add, state[first : first + (1 << b)]).astype(BF16)
                weight = tiers[i][:, inner + b : inner + b + 1]
                weighted = (weight * query[i].astype(F32)).astype(BF16)
                mixed = mixed + dot(weighted, total)
                dq = dq + weight * dot_nt(grad[i], total)
                reach = dot_tn(weighted, grad[i])
                for m in range(first, first + (1 << b)):
                    back[m] = reach if back[m] is None else back[m] + reach
            mixed_ref[span[i], col] = mixed
            dq_ref[span[i], col] = dq
            dk_ref[span[i], col] = dot_tn(dscore, query[i])
            dv_ref[span[i], col] = dot_tn(probs, grad[i])
        for i in range(count):
            if back[i] is not None:
                low = back[i].astype(BF16)
                dk_ref[span[i], col] += dot_nt(value[i], low)
                dv_ref[span[i], col] += dot(key[i], low)


def level_sums(got_refs, col, groups):
    sums, at = [], 0
    for count in groups:
        level = [ref[col, :].astype(F32) for ref in got_refs[at : at + count]]
        sums.append(functools.reduce(jnp.add, level))
        at += count
    return sums


def low_states(sums, spot_ref):
    kept = [(x * upper(spot_ref, j).astype(F32)).astype(BF16) for j, x in enumerate(sums)]
    return jnp.concatenate(kept, axis=0)


def low_back(sums, spot_ref):
    kept = [x * (1 - upper(spot_ref, j)).astype(F32) for j, x in enumerate(sums)]
    return functools.reduce(jnp.add, kept).astype(BF16)


def mixed_kernel(groups, spot_ref, mixed_ref, weighted_ref, *refs):
    got_refs, out_ref = refs[:-1], refs[-1]
    step = len(groups) * HEAD_DIM
    for i, col in enumerate(head_slices(mixed_ref.shape[1])):
        states = low_states(level_sums(got_refs, col, groups), spot_ref)
        far = dot(weighted_ref[:, i * step : (i + 1) * step], states)
        out_ref[:, col] = (mixed_ref[:, col] + far).astype(BF16)


def tail_kernel(tiers, groups, *refs):
    span = len(groups)
    place_ref, spot_ref, dq_ref, dk_ref, dv_ref, key_ref, value_ref, grad_ref, tier_ref, mixed_ref, weight_ref = refs[:11]
    got_refs = refs[11:-8]
    dq_out, dk_out, dv_out, part_ref, dq_low, dk_low, dv_low, sems = refs[-8:]
    scale = [tier_ref[:, tiers + j : tiers + j + 1] for j in range(span)]
    for col in head_slices(key_ref.shape[1]):
        sums = level_sums(got_refs, col, groups)
        back = low_back(sums, spot_ref)
        dk_low[:, col] = (dk_ref[:, col] + dot(value_ref[:, col], back)).astype(BF16)
        dv_low[:, col] = (dv_ref[:, col] + dot_nt(key_ref[:, col], back)).astype(BF16)
        far = dot_nt(grad_ref[:, col], low_states(sums, spot_ref))
        total = dq_ref[:, col]
        for j in range(span):
            total = total + scale[j] * far[:, j * HEAD_DIM : (j + 1) * HEAD_DIM]
        dq_low[:, col] = total.astype(BF16)
    copies = [
        pltpu.make_async_copy(src, dst, sems.at[n])
        for n, (src, dst) in enumerate([(dq_low, dq_out), (dk_low, dk_out), (dv_low, dv_out)])
    ]
    for copy in copies:
        copy.start()
    part_ref[...] = dot(mixed_ref[...], column(weight_ref, place_ref[0])[...])
    for copy in copies:
        copy.wait()


def layer_kernel(place_ref, part_ref, mixed_ref, weight_ref, out_hbm, out_low, sems):
    weight = column(weight_ref, place_ref[0])
    chunks = sems.shape[0]
    rows = part_ref.shape[0] // chunks
    copies = []
    for n in range(chunks):
        at = pl.ds(n * rows, rows)
        out_low[at, :] = (part_ref[at, :] + dot(mixed_ref[at, :], weight[...])).astype(BF16)
        copies.append(pltpu.make_async_copy(out_low.at[at, :], out_hbm.at[at, :], sems.at[n]))
        copies[-1].start()
    for copy in copies:
        copy.wait()


def swap_blocks(x, stride):
    return lax.ppermute(x, "seq", [(n, n ^ stride) for n in range(lax.axis_size("seq"))])


def add_low(a, b):
    return (a.astype(F32) + b.astype(F32)).astype(BF16)


def exchange_direct(sends):
    got = []
    for s in range(1, lax.axis_size("seq")):
        got.append(swap_blocks(sends[s.bit_length() - 1], s))
    return got, [1 << j for j in range(len(sends))]


def exchange_tree(state, reach, spot):
    got = []
    for j in range(len(reach)):
        from_state = swap_blocks(state, 1 << j)
        from_reach = [swap_blocks(x, 1 << j) for x in reach[j:]]
        got.append(jnp.where(spot >> j & 1 == 1, from_state, from_reach[0]))
        state = add_low(state, from_state)
        reach = reach[: j + 1] + [add_low(a, b) for a, b in zip(reach[j + 1 :], from_reach[1:])]
    return got, [1] * len(reach)


def on_device(query_in, key_in, value_in, level_mask, out_weight, grad_out):
    blocks = lax.axis_size("seq")
    span = blocks.bit_length() - 1
    if query_in.shape[0] != 1 or lax.axis_size("head") != 2 or blocks != 1 << span:
        raise ValueError("unsupported split")
    query, key, value, mask, grad = (x[0] for x in (query_in, key_in, value_in, level_mask, grad_out))
    length, width = query.shape
    half = grad.shape[1]
    tiers = length.bit_length()
    direct = blocks <= DIRECT
    place = lax.axis_index("head").astype(jnp.int32)[None]
    spot = lax.axis_index("seq").astype(jnp.int32)[None]
    swap = [(0, 1), (1, 0)]
    shape = jax.ShapeDtypeStruct
    dma = pltpu.SemaphoreType.DMA
    matrix = shape((width, HEAD_DIM), BF16)
    low = shape((length, width), BF16)
    high = shape((length, width), F32)
    low_buffer = pltpu.VMEM((length, width), BF16)
    half_buffer = pltpu.VMEM((length, half), BF16)
    unit = 2 * length * width * HEAD_DIM
    project = 2 * length * width * half

    grad_other = lax.ppermute(grad, "head", swap)
    state, part, weighted, tier = call(
        functools.partial(prep_kernel, tiers, span),
        [matrix, high, shape((length, span * width), BF16), shape((length, mask.shape[1]), F32)],
        [SMEM, VMEM] + [HBM] * 5,
        project + unit,
        (place, mask.T, *[pltpu.with_memory_space_constraint(x, pltpu.HBM) for x in (key, value, grad, out_weight, query)]),
        scratch=[low_buffer, low_buffer, half_buffer, pltpu.VMEM((width, half), BF16), low_buffer, dma((5,))],
        limit=12,
    )
    weight_other = lax.ppermute(out_weight, "head", swap)
    grad_mixed, *sends = call(
        functools.partial(reach_kernel, span, direct),
        [low] + [matrix] * span,
        [SMEM] * 2 + [VMEM] * 5,
        project + span * unit,
        (place, spot, grad_other, out_weight, part, weighted, state),
    )
    got, groups = exchange_direct(sends) if direct else exchange_tree(state, sends, spot)
    mixed, dq, dk, dv = call(local_kernel, [high] * 4, [VMEM] * 5, 12 * unit, (query, key, value, grad_mixed, tier))
    (mixed,) = call(
        functools.partial(mixed_kernel, groups),
        [low],
        [SMEM] + [VMEM] * (2 + len(got)),
        span * unit,
        (spot, mixed, weighted, *got),
    )
    mixed_other = lax.ppermute(mixed, "head", swap)
    grad_query, grad_key, grad_value, part = call(
        functools.partial(tail_kernel, tiers, groups),
        [low] * 3 + [shape((length, half), F32)],
        [SMEM] * 2 + [VMEM] * (9 + len(got)),
        project + (2 + span) * unit,
        (place, spot, dq, dk, dv, key, value, grad_mixed, tier, mixed, out_weight, *got),
        out_specs=[HBM] * 3 + [VMEM],
        scratch=[low_buffer] * 3 + [dma((3,))],
    )
    (layer_out,) = call(
        layer_kernel,
        [shape((length, half), BF16)],
        [SMEM] + [VMEM] * 3,
        project,
        (place, part, mixed_other, weight_other),
        out_specs=[HBM],
        scratch=[half_buffer, dma((4,))],
    )
    return tuple(x[None] for x in (layer_out, grad_query, grad_key, grad_value))


def solution(mesh):
    rows = P(("groups", "batch"), "seq", "head")
    return jax.shard_map(
        on_device,
        mesh=mesh,
        in_specs=(rows, rows, rows, P(("groups", "batch"), "seq", None), P("head", None), rows),
        out_specs=(rows,) * 4,
        check_vma=False,
    )
```

```python
import functools

import jax
import jax.numpy as jnp
from jax import lax
from jax.experimental import pallas as pl
from jax.experimental.pallas import tpu as pltpu
from jax.sharding import PartitionSpec as P

HEAD_DIM = 128
TILE = 256
F32 = jnp.float32
BF16 = jnp.bfloat16
VMEM = pl.BlockSpec(memory_space=pltpu.VMEM)
SMEM = pl.BlockSpec(memory_space=pltpu.SMEM)
HBM = pl.BlockSpec(memory_space=pltpu.HBM)


def level_scale(level):
    return 1.0 if level == 0 else 2.0 ** (-(level - 1) / 2.0)


def dot(a, b):
    return lax.dot_general(a, b, (((1,), (0,)), ((), ())), preferred_element_type=F32)


def dot_nt(a, b):
    return lax.dot_general(a, b, (((1,), (1,)), ((), ())), preferred_element_type=F32)


def dot_tn(a, b):
    return lax.dot_general(a, b, (((0,), (0,)), ((), ())), preferred_element_type=F32)


def call(kernel, outs, in_specs, flops, args, out_specs=None, scratch=(), limit=16):
    moved = sum(a.size * a.dtype.itemsize for a in args)
    moved += sum(o.size * o.dtype.itemsize for o in outs)
    return pl.pallas_call(
        kernel,
        out_shape=outs,
        in_specs=in_specs,
        out_specs=out_specs or [VMEM] * len(outs),
        scratch_shapes=list(scratch),
        compiler_params=pltpu.CompilerParams(vmem_limit_bytes=limit << 20),
        cost_estimate=pl.CostEstimate(flops=flops, bytes_accessed=moved, transcendentals=0),
    )(*args)


def head_slices(width):
    return [slice(i * HEAD_DIM, (i + 1) * HEAD_DIM) for i in range(width // HEAD_DIM)]


def upper(spot_ref, bit):
    return (spot_ref[0] >> bit) & 1


def column(ref, index):
    half = ref.shape[1] // 2
    return ref.at[:, pl.ds(pl.multiple_of(index * half, half), half)]


def start_copies(pairs, sems):
    copies = [pltpu.make_async_copy(src, dst, sems.at[n]) for n, (src, dst) in enumerate(pairs)]
    for copy in copies:
        copy.start()
    return copies


def state_kernel(place_ref, spot_ref, mask_hbm, key_hbm, value_hbm, grad_hbm, weight_hbm, query_hbm, *refs):
    state_ref, tier_ref, key, value, grad, weight, query, mask, sems = refs
    mine = column(weight_hbm, place_ref[0])
    sources = [key_hbm, value_hbm, mask_hbm, mine, grad_hbm, query_hbm]
    copies = start_copies(zip(sources, [key, value, mask, weight, grad, query]), sems)
    copies[0].wait()
    copies[1].wait()
    for col in head_slices(key.shape[1]):
        state_ref[col, :] = dot_tn(key[:, col], value[:, col]).astype(BF16)
    copies[2].wait()
    levels = mask[...].astype(F32)
    rows = [levels[l : l + 1] * jnp.float32(level_scale(l)) for l in range(levels.shape[0])]
    tier_ref[...] = jnp.transpose(jnp.concatenate(rows, axis=0))
    for copy in copies[3:]:
        copy.wait()


def own_kernel(tiers, span, place_ref, grad_ref, weight_ref, query_ref, tier_ref, weight_hbm, *refs):
    part_ref, weighted_ref, other_ref, sems = refs
    copies = start_copies([(column(weight_hbm, 1 - place_ref[0]), other_ref)], sems)
    part_ref[...] = dot_nt(grad_ref[...], weight_ref[...])
    length, width = query_ref.shape
    for j in range(span):
        scale = jnp.broadcast_to(tier_ref[:, tiers + j : tiers + j + 1], (length, HEAD_DIM))
        for i, col in enumerate(head_slices(width)):
            at = (i * span + j) * HEAD_DIM
            weighted_ref[:, at : at + HEAD_DIM] = (scale * query_ref[:, col].astype(F32)).astype(BF16)
    copies[0].wait()


def reach_kernel(span, spot_ref, grad_ref, weight_ref, part_ref, weighted_ref, state_ref, *outs):
    grad_mixed_ref, send_refs = outs[0], outs[1:]
    grad_mixed = (part_ref[...] + dot_nt(grad_ref[...], weight_ref[...])).astype(BF16)
    grad_mixed_ref[...] = grad_mixed
    step = span * HEAD_DIM
    for i, col in enumerate(head_slices(grad_mixed.shape[1])):
        reach = dot_tn(grad_mixed[:, col], weighted_ref[:, i * step : (i + 1) * step])
        state = state_ref[col, :].astype(F32)
        for j in range(span):
            send = jnp.where(upper(spot_ref, j) > 0, reach[:, j * HEAD_DIM : (j + 1) * HEAD_DIM], state)
            send_refs[j][col, :] = send.astype(BF16)


def add_kernel(a_ref, b_ref, out_ref):
    out_ref[...] = (a_ref[...].astype(F32) + b_ref[...].astype(F32)).astype(BF16)


def tile_blend(tier, tile):
    rows = lax.broadcasted_iota(jnp.int32, (tile, tile), 0)
    cols = lax.broadcasted_iota(jnp.int32, (tile, tile), 1)
    spread = rows ^ cols
    blend = jnp.where(spread == 0, tier[:, 0:1], 0.0)
    for level in range(1, tile.bit_length()):
        here = ((spread >> (level - 1)) == 1) & (cols < rows)
        blend = jnp.where(here, tier[:, level : level + 1], blend)
    return blend


def tiles_of(length):
    tile = min(TILE, length)
    return tile, [slice(i * tile, (i + 1) * tile) for i in range(length // tile)]


def sibling_tiles(count):
    for i in range(count):
        for b in range(count.bit_length() - 1):
            if i >> b & 1:
                first = ((i >> b) ^ 1) << b
                yield i, b, range(first, first + (1 << b))


def forward_kernel(query_ref, key_ref, value_ref, tier_ref, mixed_ref, probs_ref, blend_ref, state_ref):
    length, width = query_ref.shape
    tile, spans = tiles_of(length)
    inner = tile.bit_length()
    for rows in spans:
        blend_ref[rows, :] = tile_blend(tier_ref[rows, :], tile)
    for h, col in enumerate(head_slices(width)):
        mixed = []
        for rows in spans:
            probs = (blend_ref[rows, :] * dot_nt(query_ref[rows, col], key_ref[rows, col])).astype(BF16)
            probs_ref[rows, h * tile : (h + 1) * tile] = probs
            mixed.append(dot(probs, value_ref[rows, col]))
        states = [dot_tn(key_ref[rows, col], value_ref[rows, col]) for rows in spans[:-1]]
        for n, (i, b, members) in enumerate(sibling_tiles(len(spans))):
            total = functools.reduce(jnp.add, [states[m] for m in members]).astype(BF16)
            state_ref[n, col, :] = total
            weight = tier_ref[spans[i], inner + b : inner + b + 1]
            weighted = (weight * query_ref[spans[i], col].astype(F32)).astype(BF16)
            mixed[i] = mixed[i] + dot(weighted, total)
        for rows, value in zip(spans, mixed):
            mixed_ref[rows, col] = value


def backward_kernel(query_ref, key_ref, value_ref, grad_ref, tier_ref, probs_ref, blend_ref, state_ref, *outs):
    dq_ref, dk_ref, dv_ref = outs
    length, width = query_ref.shape
    tile, spans = tiles_of(length)
    inner = tile.bit_length()
    for h, col in enumerate(head_slices(width)):
        dq, dk, dv = [], [], []
        for rows in spans:
            query, key, value, grad = (ref[rows, col] for ref in (query_ref, key_ref, value_ref, grad_ref))
            dscore = (blend_ref[rows, :] * dot_nt(grad, value)).astype(BF16)
            dq.append(dot(dscore, key))
            dk.append(dot_tn(dscore, query))
            dv.append(dot_tn(probs_ref[rows, h * tile : (h + 1) * tile], grad))
        backs = [None] * len(spans)
        for n, (i, b, members) in enumerate(sibling_tiles(len(spans))):
            grad = grad_ref[spans[i], col]
            weight = tier_ref[spans[i], inner + b : inner + b + 1]
            weighted = (weight * query_ref[spans[i], col].astype(F32)).astype(BF16)
            dq[i] = dq[i] + weight * dot_nt(grad, state_ref[n, col, :])
            reach = dot_tn(grad, weighted)
            for m in members:
                backs[m] = reach if backs[m] is None else backs[m] + reach
        for m, rows in enumerate(spans):
            if backs[m] is not None:
                low = backs[m].astype(BF16)
                dk[m] = dk[m] + dot(value_ref[rows, col], low)
                dv[m] = dv[m] + dot_nt(key_ref[rows, col], low)
            dq_ref[rows, col] = dq[m]
            dk_ref[rows, col] = dk[m]
            dv_ref[rows, col] = dv[m]


def low_states(state_refs, col, spot_ref):
    kept = [(ref[col, :].astype(F32) * upper(spot_ref, j).astype(F32)).astype(BF16) for j, ref in enumerate(state_refs)]
    return jnp.concatenate(kept, axis=0)


def low_back(back_refs, col, spot_ref):
    kept = [ref[col, :].astype(F32) * (1 - upper(spot_ref, j)).astype(F32) for j, ref in enumerate(back_refs)]
    return functools.reduce(jnp.add, kept).astype(BF16)


def mixed_kernel(spot_ref, mixed_ref, weighted_ref, *refs):
    state_refs, out_ref = refs[:-1], refs[-1]
    step = len(state_refs) * HEAD_DIM
    for i, col in enumerate(head_slices(mixed_ref.shape[1])):
        far = dot(weighted_ref[:, i * step : (i + 1) * step], low_states(state_refs, col, spot_ref))
        out_ref[:, col] = (mixed_ref[:, col] + far).astype(BF16)


def query_kernel(tiers, span, spot_ref, dq_ref, dk_ref, dv_ref, key_ref, value_ref, grad_ref, tier_ref, *refs):
    mixed_ref, weight_ref = refs[:2]
    got_refs = refs[2:-4]
    dq_low, dk_low, dv_low, part_ref = refs[-4:]
    scale = [tier_ref[:, tiers + j : tiers + j + 1] for j in range(span)]
    for col in head_slices(dq_ref.shape[1]):
        far = dot_nt(grad_ref[:, col], low_states(got_refs, col, spot_ref))
        total = dq_ref[:, col]
        for j in range(span):
            total = total + scale[j] * far[:, j * HEAD_DIM : (j + 1) * HEAD_DIM]
        dq_low[:, col] = total.astype(BF16)
        back = low_back(got_refs, col, spot_ref)
        dk_low[:, col] = (dk_ref[:, col] + dot(value_ref[:, col], back)).astype(BF16)
        dv_low[:, col] = (dv_ref[:, col] + dot_nt(key_ref[:, col], back)).astype(BF16)
    part_ref[...] = dot(mixed_ref[...], weight_ref[...])


def last_kernel(part_ref, mixed_ref, weight_ref, dq_low, dk_low, dv_low, out_hbm, dq_hbm, dk_hbm, dv_hbm, out_low, sems):
    chunks = sems.shape[0] - 3
    rows = part_ref.shape[0] // chunks
    copies = []

    def send(src, dst):
        copies.append(pltpu.make_async_copy(src, dst, sems.at[len(copies)]))
        copies[-1].start()

    send(dq_low, dq_hbm)
    send(dk_low, dk_hbm)
    send(dv_low, dv_hbm)
    for n in range(chunks):
        at = pl.ds(n * rows, rows)
        out_low[at, :] = (part_ref[at, :] + dot(mixed_ref[at, :], weight_ref[...])).astype(BF16)
        send(out_low.at[at, :], out_hbm.at[at, :])
    for copy in copies:
        copy.wait()


def swap_blocks(x, level):
    return lax.ppermute(x, "seq", [(n, n ^ 1 << level) for n in range(lax.axis_size("seq"))])


def add_low(a, b):
    return call(add_kernel, [jax.ShapeDtypeStruct(a.shape, BF16)], [VMEM] * 2, a.size, (a, b), limit=4)[0]


def hbm(*arrays):
    return [pltpu.with_memory_space_constraint(x, pltpu.HBM) for x in arrays]


def on_device(query_in, key_in, value_in, level_mask, out_weight, grad_out):
    blocks = lax.axis_size("seq")
    span = blocks.bit_length() - 1
    if query_in.shape[0] != 1 or lax.axis_size("head") != 2 or blocks != 1 << span:
        raise ValueError("unsupported split")
    query, key, value, mask, grad = (x[0] for x in (query_in, key_in, value_in, level_mask, grad_out))
    length, width = query.shape
    half = grad.shape[1]
    tiers = length.bit_length()
    tile, spans = tiles_of(length)
    siblings = max(1, len(list(sibling_tiles(len(spans)))))
    place = lax.axis_index("head").astype(jnp.int32)[None]
    spot = lax.axis_index("seq").astype(jnp.int32)[None]
    swap = [(0, 1), (1, 0)]
    shape = jax.ShapeDtypeStruct
    dma = pltpu.SemaphoreType.DMA
    matrix = shape((width, HEAD_DIM), BF16)
    low = shape((length, width), BF16)
    high = shape((length, width), F32)
    wide = shape((length, half), BF16)
    low_buffer = pltpu.VMEM((length, width), BF16)
    unit = 2 * length * width * HEAD_DIM
    project = 2 * length * width * half

    grad_other = lax.ppermute(grad, "head", swap)
    state, tier, key, value, grad_own, weight_own, query = call(
        state_kernel,
        [matrix, shape((length, mask.shape[1]), F32), low, low, wide, shape((width, half), BF16), low],
        [SMEM] * 2 + [HBM] * 6,
        unit,
        (place, spot, *hbm(mask.T, key, value, grad, out_weight, query)),
        scratch=[pltpu.VMEM(mask.shape[::-1], mask.dtype), dma((6,))],
    )
    part, weighted, weight_rest = call(
        functools.partial(own_kernel, tiers, span),
        [high, shape((length, span * width), BF16), shape((width, half), BF16)],
        [SMEM] + [VMEM] * 4 + [HBM],
        project,
        (place, grad_own, weight_own, query, tier, *hbm(out_weight)),
        scratch=[dma((1,))],
    )
    grad_mixed, *sends = call(
        functools.partial(reach_kernel, span),
        [low] + [matrix] * span,
        [SMEM] + [VMEM] * 5,
        project + span * unit,
        (spot, grad_other, weight_rest, part, weighted, state),
    )
    weight_other = lax.ppermute(weight_rest, "head", swap)
    mixed, probs, blend, inner = call(
        forward_kernel,
        [high, shape((length, width // HEAD_DIM * tile), BF16), shape((length, tile), F32)]
        + [shape((siblings, width, HEAD_DIM), BF16)],
        [VMEM] * 4,
        4 * unit,
        (query, key, value, tier),
    )
    got = []
    for level, total in enumerate(sends):
        for step in range(level):
            total = add_low(total, swap_blocks(total, step))
        got.append(swap_blocks(total, level))
    dq, dk, dv = call(
        backward_kernel, [high] * 3, [VMEM] * 8, 8 * unit, (query, key, value, grad_mixed, tier, probs, blend, inner)
    )
    (mixed,) = call(mixed_kernel, [low], [SMEM] + [VMEM] * (2 + span), span * unit, (spot, mixed, weighted, *got))
    mixed_other = lax.ppermute(mixed, "head", swap)
    *lows, part = call(
        functools.partial(query_kernel, tiers, span),
        [low] * 3 + [shape((length, half), F32)],
        [SMEM] + [VMEM] * (9 + span),
        project + (2 + span) * unit,
        (spot, dq, dk, dv, key, value, grad_mixed, tier, mixed, weight_own, *got),
    )
    layer_out, grad_query, grad_key, grad_value = call(
        last_kernel,
        [wide, low, low, low],
        [VMEM] * 6,
        project,
        (part, mixed_other, weight_other, *lows),
        out_specs=[HBM] * 4,
        scratch=[pltpu.VMEM((length, half), BF16), dma((7,))],
    )
    return tuple(x[None] for x in (layer_out, grad_query, grad_key, grad_value))


def solution(mesh):
    rows = P(("groups", "batch"), "seq", "head")
    return jax.shard_map(
        on_device,
        mesh=mesh,
        in_specs=(rows, rows, rows, P(("groups", "batch"), "seq", None), P("head", None), rows),
        out_specs=(rows,) * 4,
        check_vma=False,
    )
```

```python
import functools

import jax
import jax.numpy as jnp
from jax import lax
from jax.experimental import pallas as pl
from jax.experimental.pallas import tpu as pltpu
from jax.sharding import PartitionSpec as P

HEAD_DIM = 128
TILE = 256
F32 = jnp.float32
BF16 = jnp.bfloat16
VMEM = pl.BlockSpec(memory_space=pltpu.VMEM)
SMEM = pl.BlockSpec(memory_space=pltpu.SMEM)
HBM = pl.BlockSpec(memory_space=pltpu.HBM)


def level_scale(level):
    return 1.0 if level == 0 else 2.0 ** (-(level - 1) / 2.0)


def dot(a, b):
    return lax.dot_general(a, b, (((1,), (0,)), ((), ())), preferred_element_type=F32)


def dot_nt(a, b):
    return lax.dot_general(a, b, (((1,), (1,)), ((), ())), preferred_element_type=F32)


def dot_tn(a, b):
    return lax.dot_general(a, b, (((0,), (0,)), ((), ())), preferred_element_type=F32)


def call(kernel, outs, in_specs, flops, args, out_specs=None, scratch=(), limit=16, aliases=None):
    moved = sum(a.size * a.dtype.itemsize for a in args)
    moved += sum(o.size * o.dtype.itemsize for o in outs)
    return pl.pallas_call(
        kernel,
        out_shape=outs,
        in_specs=in_specs,
        out_specs=out_specs or [VMEM] * len(outs),
        scratch_shapes=list(scratch),
        input_output_aliases=aliases or {},
        compiler_params=pltpu.CompilerParams(vmem_limit_bytes=limit << 20),
        cost_estimate=pl.CostEstimate(flops=flops, bytes_accessed=moved, transcendentals=0),
    )(*args)


def head_slices(width):
    return [slice(i * HEAD_DIM, (i + 1) * HEAD_DIM) for i in range(width // HEAD_DIM)]


def upper(spot_ref, bit):
    return (spot_ref[0] >> bit) & 1


def column(ref, index):
    half = ref.shape[1] // 2
    return ref.at[:, pl.ds(pl.multiple_of(index * half, half), half)]


def start_copies(pairs, sems):
    copies = [pltpu.make_async_copy(src, dst, sems.at[n]) for n, (src, dst) in enumerate(pairs)]
    for copy in copies:
        copy.start()
    return copies


def prep_kernel(tiers, span, place_ref, spot_ref, mask_hbm, key_hbm, value_hbm, grad_hbm, weight_hbm, query_hbm, *refs):
    state_ref, tier_ref, key, value, weight, rest, query, part_ref, weighted_ref, mask, grad, sems = refs
    mine, other = column(weight_hbm, place_ref[0]), column(weight_hbm, 1 - place_ref[0])
    sources = [mine, grad_hbm, key_hbm, value_hbm, mask_hbm, query_hbm, other]
    copies = start_copies(zip(sources, [weight, grad, key, value, mask, query, rest]), sems)
    copies[0].wait()
    copies[1].wait()
    part_ref[...] = dot_nt(grad[...], weight[...])
    copies[2].wait()
    copies[3].wait()
    cols = head_slices(key.shape[1])
    for col in cols:
        state_ref[col, :] = dot_tn(key[:, col], value[:, col]).astype(BF16)
    copies[4].wait()
    levels = mask[...].astype(F32)
    rows = [levels[l : l + 1] * jnp.float32(level_scale(l)) for l in range(levels.shape[0])]
    tier = jnp.transpose(jnp.concatenate(rows, axis=0))
    tier_ref[...] = tier
    copies[5].wait()
    for j in range(span):
        scale = jnp.broadcast_to(tier[:, tiers + j : tiers + j + 1], (tier.shape[0], HEAD_DIM))
        for i, col in enumerate(cols):
            at = (i * span + j) * HEAD_DIM
            weighted_ref[:, at : at + HEAD_DIM] = (scale * query[:, col].astype(F32)).astype(BF16)
    copies[6].wait()


def reach_kernel(span, spot_ref, grad_ref, weight_ref, part_ref, weighted_ref, state_ref, *outs):
    grad_mixed_ref, send_refs = outs[0], outs[1:]
    grad_mixed = (part_ref[...] + dot_nt(grad_ref[...], weight_ref[...])).astype(BF16)
    grad_mixed_ref[...] = grad_mixed
    step = span * HEAD_DIM
    for i, col in enumerate(head_slices(grad_mixed.shape[1])):
        reach = dot_tn(grad_mixed[:, col], weighted_ref[:, i * step : (i + 1) * step])
        state = state_ref[col, :].astype(F32)
        for j in range(span):
            send = jnp.where(upper(spot_ref, j) > 0, reach[:, j * HEAD_DIM : (j + 1) * HEAD_DIM], state)
            send_refs[j][col, :] = send.astype(BF16)


def add_kernel(a_ref, b_ref, out_ref):
    out_ref[...] = (a_ref[...].astype(F32) + b_ref[...].astype(F32)).astype(BF16)


def tile_blend(tier, tile):
    rows = lax.broadcasted_iota(jnp.int32, (tile, tile), 0)
    cols = lax.broadcasted_iota(jnp.int32, (tile, tile), 1)
    spread = rows ^ cols
    blend = jnp.where(spread == 0, tier[:, 0:1], 0.0)
    for level in range(1, tile.bit_length()):
        here = ((spread >> (level - 1)) == 1) & (cols < rows)
        blend = jnp.where(here, tier[:, level : level + 1], blend)
    return blend


def tiles_of(length):
    tile = min(TILE, length)
    return tile, [slice(i * tile, (i + 1) * tile) for i in range(length // tile)]


def sibling_tiles(count):
    for i in range(count):
        for b in range(count.bit_length() - 1):
            if i >> b & 1:
                first = ((i >> b) ^ 1) << b
                yield i, b, range(first, first + (1 << b))


def forward_kernel(query_ref, key_ref, value_ref, tier_ref, mixed_ref, probs_ref, blend_ref, state_ref):
    length, width = query_ref.shape
    tile, spans = tiles_of(length)
    inner = tile.bit_length()
    for rows in spans:
        blend_ref[rows, :] = tile_blend(tier_ref[rows, :], tile)
    for h, col in enumerate(head_slices(width)):
        mixed = []
        for rows in spans:
            probs = (blend_ref[rows, :] * dot_nt(query_ref[rows, col], key_ref[rows, col])).astype(BF16)
            probs_ref[rows, h * tile : (h + 1) * tile] = probs
            mixed.append(dot(probs, value_ref[rows, col]))
        states = [dot_tn(key_ref[rows, col], value_ref[rows, col]) for rows in spans[:-1]]
        for n, (i, b, members) in enumerate(sibling_tiles(len(spans))):
            total = functools.reduce(jnp.add, [states[m] for m in members]).astype(BF16)
            state_ref[n, col, :] = total
            weight = tier_ref[spans[i], inner + b : inner + b + 1]
            weighted = (weight * query_ref[spans[i], col].astype(F32)).astype(BF16)
            mixed[i] = mixed[i] + dot(weighted, total)
        for rows, value in zip(spans, mixed):
            mixed_ref[rows, col] = value


def backward_kernel(query_ref, key_ref, value_ref, grad_ref, tier_ref, probs_ref, blend_ref, state_ref, *outs):
    dq_ref, dk_ref, dv_ref = outs
    length, width = query_ref.shape
    tile, spans = tiles_of(length)
    inner = tile.bit_length()
    for h, col in enumerate(head_slices(width)):
        dq, dk, dv = [], [], []
        for rows in spans:
            query, key, value, grad = (ref[rows, col] for ref in (query_ref, key_ref, value_ref, grad_ref))
            dscore = (blend_ref[rows, :] * dot_nt(grad, value)).astype(BF16)
            dq.append(dot(dscore, key))
            dk.append(dot_tn(dscore, query))
            dv.append(dot_tn(probs_ref[rows, h * tile : (h + 1) * tile], grad))
        backs = [None] * len(spans)
        for n, (i, b, members) in enumerate(sibling_tiles(len(spans))):
            grad = grad_ref[spans[i], col]
            weight = tier_ref[spans[i], inner + b : inner + b + 1]
            weighted = (weight * query_ref[spans[i], col].astype(F32)).astype(BF16)
            dq[i] = dq[i] + weight * dot_nt(grad, state_ref[n, col, :])
            reach = dot_tn(grad, weighted)
            for m in members:
                backs[m] = reach if backs[m] is None else backs[m] + reach
        for m, rows in enumerate(spans):
            if backs[m] is not None:
                low = backs[m].astype(BF16)
                dk[m] = dk[m] + dot(value_ref[rows, col], low)
                dv[m] = dv[m] + dot_nt(key_ref[rows, col], low)
            dq_ref[rows, col] = dq[m]
            dk_ref[rows, col] = dk[m]
            dv_ref[rows, col] = dv[m]


def low_states(state_refs, col, spot_ref):
    kept = [(ref[col, :].astype(F32) * upper(spot_ref, j).astype(F32)).astype(BF16) for j, ref in enumerate(state_refs)]
    return jnp.concatenate(kept, axis=0)


def low_back(back_refs, col, spot_ref):
    kept = [ref[col, :].astype(F32) * (1 - upper(spot_ref, j)).astype(F32) for j, ref in enumerate(back_refs)]
    return functools.reduce(jnp.add, kept).astype(BF16)


def far(spot_ref, top):
    return upper(spot_ref, top) > 0


def near_mixed_kernel(span, spot_ref, mixed_ref, weighted_ref, *refs):
    got_refs, out_ref = refs[:-1], refs[-1]
    for i, col in enumerate(head_slices(mixed_ref.shape[1])):
        total = mixed_ref[:, col]
        if got_refs:
            at = i * span * HEAD_DIM
            weighted = weighted_ref[:, at : at + len(got_refs) * HEAD_DIM]
            total = total + dot(weighted, low_states(got_refs, col, spot_ref))
        out_ref[:, col] = total.astype(BF16)


def far_mixed_kernel(spot_ref, mixed_ref, weighted_ref, *refs):
    got_refs, out_ref = refs[:-1], refs[-1]
    step = len(got_refs) * HEAD_DIM

    @pl.when(far(spot_ref, len(got_refs) - 1))
    def _():
        for i, col in enumerate(head_slices(mixed_ref.shape[1])):
            total = dot(weighted_ref[:, i * step : (i + 1) * step], low_states(got_refs, col, spot_ref))
            out_ref[:, col] = (mixed_ref[:, col] + total).astype(BF16)


def near_own_kernel(tiers, top, spot_ref, dq_ref, grad_ref, tier_ref, mixed_ref, weight_ref, *refs):
    got_refs, (near_dq_ref, part_ref) = refs[:-2], refs[-2:]
    for col in head_slices(dq_ref.shape[1]):
        total = dq_ref[:, col]
        if got_refs:
            rest = dot_nt(grad_ref[:, col], low_states(got_refs, col, spot_ref))
            for j in range(top):
                scale = tier_ref[:, tiers + j : tiers + j + 1]
                total = total + scale * rest[:, j * HEAD_DIM : (j + 1) * HEAD_DIM]
        near_dq_ref[:, col] = total

    @pl.when(jnp.logical_not(far(spot_ref, top)))
    def _():
        part_ref[...] = dot(mixed_ref[...], weight_ref[...])


def near_layer_kernel(top, spot_ref, part_ref, mixed_ref, weight_ref, out_ref):
    @pl.when(jnp.logical_not(far(spot_ref, top)))
    def _():
        out_ref[...] = (part_ref[...] + dot(mixed_ref[...], weight_ref[...])).astype(BF16)


def finish_kernel(tiers, spot_ref, dk_ref, dv_ref, key_ref, value_ref, near_dq_ref, grad_ref, tier_ref, *refs):
    mixed_ref, weight_ref, layer_ref = refs[:3]
    got_refs = refs[3:-10]
    out_hbm, dq_hbm, dk_hbm, dv_hbm, part_ref, dq_low, dk_low, dv_low, near_low, sems = refs[-10:]
    top = len(got_refs) - 1
    cols = head_slices(key_ref.shape[1])
    near = jnp.logical_not(far(spot_ref, top))
    early = [pltpu.make_async_copy(layer_ref, out_hbm, sems.at[0]), pltpu.make_async_copy(near_low, dq_hbm, sems.at[1])]
    late = [pltpu.make_async_copy(dk_low, dk_hbm, sems.at[2]), pltpu.make_async_copy(dv_low, dv_hbm, sems.at[3])]

    @pl.when(near)
    def _():
        early[0].start()
        near_low[...] = near_dq_ref[...].astype(BF16)
        early[1].start()

    for col in cols:
        back = low_back(got_refs, col, spot_ref)
        dk_low[:, col] = (dk_ref[:, col] + dot(value_ref[:, col], back)).astype(BF16)
        dv_low[:, col] = (dv_ref[:, col] + dot_nt(key_ref[:, col], back)).astype(BF16)

    @pl.when(near)
    def _():
        for copy in late:
            copy.start()
        for copy in early + late:
            copy.wait()

    @pl.when(far(spot_ref, top))
    def _():
        part_ref[...] = dot(mixed_ref[...], weight_ref[...])
        scale = tier_ref[:, tiers + top : tiers + top + 1]
        for col in cols:
            rest = dot_nt(grad_ref[:, col], got_refs[top][col, :])
            dq_low[:, col] = (near_dq_ref[:, col] + scale * rest).astype(BF16)


def far_layer_kernel(top, spot_ref, part_ref, mixed_ref, weight_ref, dq_ref, dk_ref, dv_ref, *refs):
    outs, (out_low, sems) = refs[4:8], refs[8:]

    @pl.when(far(spot_ref, top))
    def _():
        copies = start_copies(zip([dq_ref, dk_ref, dv_ref], outs[1:]), sems)
        chunks = sems.shape[0] - len(copies)
        rows = part_ref.shape[0] // chunks
        for n in range(chunks):
            at = pl.ds(n * rows, rows)
            out_low[at, :] = (part_ref[at, :] + dot(mixed_ref[at, :], weight_ref[...])).astype(BF16)
            copies.append(pltpu.make_async_copy(out_low.at[at, :], outs[0].at[at, :], sems.at[len(copies)]))
            copies[-1].start()
        for copy in copies:
            copy.wait()


def swap_blocks(x, level):
    return lax.ppermute(x, "seq", [(n, n ^ 1 << level) for n in range(lax.axis_size("seq"))])


def add_low(a, b):
    return call(add_kernel, [jax.ShapeDtypeStruct(a.shape, BF16)], [VMEM] * 2, a.size, (a, b), limit=4)[0]


def hbm(*arrays):
    return [pltpu.with_memory_space_constraint(x, pltpu.HBM) for x in arrays]


def on_device(query_in, key_in, value_in, level_mask, out_weight, grad_out):
    blocks = lax.axis_size("seq")
    span = blocks.bit_length() - 1
    if query_in.shape[0] != 1 or lax.axis_size("head") != 2 or blocks != 1 << span:
        raise ValueError("unsupported split")
    query, key, value, mask, grad = (x[0] for x in (query_in, key_in, value_in, level_mask, grad_out))
    length, width = query.shape
    half = grad.shape[1]
    tiers = length.bit_length()
    tile, spans = tiles_of(length)
    siblings = max(1, len(list(sibling_tiles(len(spans)))))
    place = lax.axis_index("head").astype(jnp.int32)[None]
    spot = lax.axis_index("seq").astype(jnp.int32)[None]
    swap = [(0, 1), (1, 0)]
    shape = jax.ShapeDtypeStruct
    dma = pltpu.SemaphoreType.DMA
    matrix = shape((width, HEAD_DIM), BF16)
    low = shape((length, width), BF16)
    high = shape((length, width), F32)
    wide = shape((length, half), BF16)
    low_buffer = pltpu.VMEM((length, width), BF16)
    unit = 2 * length * width * HEAD_DIM
    project = 2 * length * width * half

    grad_other = lax.ppermute(grad, "head", swap)
    state, tier, key, value, weight_own, weight_rest, query, part, weighted = call(
        functools.partial(prep_kernel, tiers, span),
        [matrix, shape((length, mask.shape[1]), F32), low, low]
        + [shape((width, half), BF16)] * 2
        + [low, high, shape((length, span * width), BF16)],
        [SMEM] * 2 + [HBM] * 6,
        project + unit,
        (place, spot, *hbm(mask.T, key, value, grad, out_weight, query)),
        scratch=[pltpu.VMEM(mask.shape[::-1], mask.dtype), pltpu.VMEM((length, half), BF16), dma((7,))],
    )
    grad_mixed, *sends = call(
        functools.partial(reach_kernel, span),
        [low] + [matrix] * span,
        [SMEM] + [VMEM] * 5,
        project + span * unit,
        (spot, grad_other, weight_rest, part, weighted, state),
    )
    weight_other = lax.ppermute(weight_rest, "head", swap)
    mixed, probs, blend, inner = call(
        forward_kernel,
        [high, shape((length, width // HEAD_DIM * tile), BF16), shape((length, tile), F32)]
        + [shape((siblings, width, HEAD_DIM), BF16)],
        [VMEM] * 4,
        4 * unit,
        (query, key, value, tier),
    )
    got = []
    for level, total in enumerate(sends):
        for step in range(level):
            total = add_low(total, swap_blocks(total, step))
        got.append(swap_blocks(total, level))
    dq, dk, dv = call(
        backward_kernel, [high] * 3, [VMEM] * 8, 8 * unit, (query, key, value, grad_mixed, tier, probs, blend, inner)
    )
    top = span - 1
    (near_mixed,) = call(
        functools.partial(near_mixed_kernel, span),
        [low],
        [SMEM] + [VMEM] * (2 + top),
        top * unit,
        (spot, mixed, weighted, *got[:top]),
    )
    near_other = lax.ppermute(near_mixed, "head", swap)
    near_dq, part = call(
        functools.partial(near_own_kernel, tiers, top),
        [high, shape((length, half), F32)],
        [SMEM] + [VMEM] * (5 + top),
        project + top * unit,
        (spot, dq, grad_mixed, tier, near_mixed, weight_own, *got[:top]),
    )
    (near_layer,) = call(
        functools.partial(near_layer_kernel, top),
        [wide],
        [SMEM] + [VMEM] * 3,
        project,
        (spot, part, near_other, weight_other),
    )
    (mixed,) = call(far_mixed_kernel, [low], [SMEM] + [VMEM] * (2 + span), span * unit, (spot, mixed, weighted, *got))
    mixed_other = lax.ppermute(mixed, "head", swap)
    *outs, part, dq_low, dk_low, dv_low = call(
        functools.partial(finish_kernel, tiers),
        [wide, low, low, low, shape((length, half), F32), low, low, low],
        [SMEM] + [VMEM] * (10 + span),
        project + 3 * unit,
        (spot, dk, dv, key, value, near_dq, grad_mixed, tier, mixed, weight_own, near_layer, *got),
        out_specs=[HBM] * 4 + [VMEM] * 4,
        scratch=[low_buffer, dma((4,))],
    )
    layer_out, grad_query, grad_key, grad_value = call(
        functools.partial(far_layer_kernel, top),
        [wide, low, low, low],
        [SMEM] + [VMEM] * 6 + [HBM] * 4,
        project,
        (spot, part, mixed_other, weight_other, dq_low, dk_low, dv_low, *outs),
        out_specs=[HBM] * 4,
        scratch=[pltpu.VMEM((length, half), BF16), dma((7,))],
        aliases={7 + n: n for n in range(4)},
    )
    return tuple(x[None] for x in (layer_out, grad_query, grad_key, grad_value))


def solution(mesh):
    rows = P(("groups", "batch"), "seq", "head")
    return jax.shard_map(
        on_device,
        mesh=mesh,
        in_specs=(rows, rows, rows, P(("groups", "batch"), "seq", None), P("head", None), rows),
        out_specs=(rows,) * 4,
        check_vma=False,
    )
```

```python
import functools

import jax
import jax.numpy as jnp
from jax import lax
from jax.experimental import pallas as pl
from jax.experimental.pallas import tpu as pltpu
from jax.sharding import PartitionSpec as P

HEAD_DIM = 128
TILE = 256
F32 = jnp.float32
BF16 = jnp.bfloat16
VMEM = pl.BlockSpec(memory_space=pltpu.VMEM)
SMEM = pl.BlockSpec(memory_space=pltpu.SMEM)
HBM = pl.BlockSpec(memory_space=pltpu.HBM)


def level_scale(level):
    return 1.0 if level == 0 else 2.0 ** (-(level - 1) / 2.0)


def dot(a, b):
    return lax.dot_general(a, b, (((1,), (0,)), ((), ())), preferred_element_type=F32)


def dot_nt(a, b):
    return lax.dot_general(a, b, (((1,), (1,)), ((), ())), preferred_element_type=F32)


def dot_tn(a, b):
    return lax.dot_general(a, b, (((0,), (0,)), ((), ())), preferred_element_type=F32)


def call(kernel, outs, in_specs, flops, args, out_specs=None, scratch=(), limit=16, aliases=None):
    moved = sum(a.size * a.dtype.itemsize for a in args)
    moved += sum(o.size * o.dtype.itemsize for o in outs)
    return pl.pallas_call(
        kernel,
        out_shape=outs,
        in_specs=in_specs,
        out_specs=out_specs or [VMEM] * len(outs),
        scratch_shapes=list(scratch),
        input_output_aliases=aliases or {},
        compiler_params=pltpu.CompilerParams(vmem_limit_bytes=limit << 20),
        cost_estimate=pl.CostEstimate(flops=flops, bytes_accessed=moved, transcendentals=0),
    )(*args)


def head_slices(width):
    return [slice(i * HEAD_DIM, (i + 1) * HEAD_DIM) for i in range(width // HEAD_DIM)]


def upper(spot_ref, bit):
    return (spot_ref[0] >> bit) & 1


def column(ref, index):
    half = ref.shape[1] // 2
    return ref.at[:, pl.ds(pl.multiple_of(index * half, half), half)]


def start_copies(pairs, sems):
    copies = [pltpu.make_async_copy(src, dst, sems.at[n]) for n, (src, dst) in enumerate(pairs)]
    for copy in copies:
        copy.start()
    return copies


def prep_kernel(tiers, span, place_ref, spot_ref, mask_hbm, key_hbm, value_hbm, grad_hbm, weight_hbm, query_hbm, *refs):
    state_ref, tier_ref, key, value, weight, rest, query, part_ref, weighted_ref, mask, grad, sems = refs
    mine, other = column(weight_hbm, place_ref[0]), column(weight_hbm, 1 - place_ref[0])
    sources = [mine, grad_hbm, key_hbm, value_hbm, mask_hbm, query_hbm, other]
    copies = start_copies(zip(sources, [weight, grad, key, value, mask, query, rest]), sems)
    copies[0].wait()
    copies[1].wait()
    part_ref[...] = dot_nt(grad[...], weight[...])
    copies[2].wait()
    copies[3].wait()
    cols = head_slices(key.shape[1])
    for col in cols:
        state_ref[col, :] = dot_tn(key[:, col], value[:, col]).astype(BF16)
    copies[4].wait()
    levels = mask[...].astype(F32)
    rows = [levels[l : l + 1] * jnp.float32(level_scale(l)) for l in range(levels.shape[0])]
    tier = jnp.transpose(jnp.concatenate(rows, axis=0))
    tier_ref[...] = tier
    copies[5].wait()
    for j in range(span):
        scale = jnp.broadcast_to(tier[:, tiers + j : tiers + j + 1], (tier.shape[0], HEAD_DIM))
        for i, col in enumerate(cols):
            at = (i * span + j) * HEAD_DIM
            weighted_ref[:, at : at + HEAD_DIM] = (scale * query[:, col].astype(F32)).astype(BF16)
    copies[6].wait()


def reach_kernel(span, spot_ref, grad_ref, weight_ref, part_ref, weighted_ref, state_ref, *outs):
    grad_mixed_ref, send_refs = outs[0], outs[1:]
    grad_mixed = (part_ref[...] + dot_nt(grad_ref[...], weight_ref[...])).astype(BF16)
    grad_mixed_ref[...] = grad_mixed
    step = span * HEAD_DIM
    for i, col in enumerate(head_slices(grad_mixed.shape[1])):
        reach = dot_tn(grad_mixed[:, col], weighted_ref[:, i * step : (i + 1) * step])
        state = state_ref[col, :].astype(F32)
        for j in range(span):
            send = jnp.where(upper(spot_ref, j) > 0, reach[:, j * HEAD_DIM : (j + 1) * HEAD_DIM], state)
            send_refs[j][col, :] = send.astype(BF16)


def add_kernel(a_ref, b_ref, out_ref):
    out_ref[...] = (a_ref[...].astype(F32) + b_ref[...].astype(F32)).astype(BF16)


def tile_blend(tier, tile):
    rows = lax.broadcasted_iota(jnp.int32, (tile, tile), 0)
    cols = lax.broadcasted_iota(jnp.int32, (tile, tile), 1)
    spread = rows ^ cols
    blend = jnp.where(spread == 0, tier[:, 0:1], 0.0)
    for level in range(1, tile.bit_length()):
        here = ((spread >> (level - 1)) == 1) & (cols < rows)
        blend = jnp.where(here, tier[:, level : level + 1], blend)
    return blend


def tiles_of(length):
    tile = min(TILE, length)
    return tile, [slice(i * tile, (i + 1) * tile) for i in range(length // tile)]


def sibling_tiles(count):
    for i in range(count):
        for b in range(count.bit_length() - 1):
            if i >> b & 1:
                first = ((i >> b) ^ 1) << b
                yield i, b, range(first, first + (1 << b))


def forward_kernel(query_ref, key_ref, value_ref, tier_ref, mixed_ref, probs_ref, blend_ref, state_ref):
    length, width = query_ref.shape
    tile, spans = tiles_of(length)
    inner = tile.bit_length()
    for rows in spans:
        blend_ref[rows, :] = tile_blend(tier_ref[rows, :], tile)
    for h, col in enumerate(head_slices(width)):
        mixed = []
        for rows in spans:
            probs = (blend_ref[rows, :] * dot_nt(query_ref[rows, col], key_ref[rows, col])).astype(BF16)
            probs_ref[rows, h * tile : (h + 1) * tile] = probs
            mixed.append(dot(probs, value_ref[rows, col]))
        states = [dot_tn(key_ref[rows, col], value_ref[rows, col]) for rows in spans[:-1]]
        for n, (i, b, members) in enumerate(sibling_tiles(len(spans))):
            total = functools.reduce(jnp.add, [states[m] for m in members]).astype(BF16)
            state_ref[n, col, :] = total
            weight = tier_ref[spans[i], inner + b : inner + b + 1]
            weighted = (weight * query_ref[spans[i], col].astype(F32)).astype(BF16)
            mixed[i] = mixed[i] + dot(weighted, total)
        for rows, value in zip(spans, mixed):
            mixed_ref[rows, col] = value


def backward_kernel(query_ref, key_ref, value_ref, grad_ref, tier_ref, probs_ref, blend_ref, state_ref, *outs):
    dq_ref, dk_ref, dv_ref = outs
    length, width = query_ref.shape
    tile, spans = tiles_of(length)
    inner = tile.bit_length()
    for h, col in enumerate(head_slices(width)):
        dq, dk, dv = [], [], []
        for rows in spans:
            query, key, value, grad = (ref[rows, col] for ref in (query_ref, key_ref, value_ref, grad_ref))
            dscore = (blend_ref[rows, :] * dot_nt(grad, value)).astype(BF16)
            dq.append(dot(dscore, key))
            dk.append(dot_tn(dscore, query))
            dv.append(dot_tn(probs_ref[rows, h * tile : (h + 1) * tile], grad))
        backs = [None] * len(spans)
        for n, (i, b, members) in enumerate(sibling_tiles(len(spans))):
            grad = grad_ref[spans[i], col]
            weight = tier_ref[spans[i], inner + b : inner + b + 1]
            weighted = (weight * query_ref[spans[i], col].astype(F32)).astype(BF16)
            dq[i] = dq[i] + weight * dot_nt(grad, state_ref[n, col, :])
            reach = dot_tn(grad, weighted)
            for m in members:
                backs[m] = reach if backs[m] is None else backs[m] + reach
        for m, rows in enumerate(spans):
            if backs[m] is not None:
                low = backs[m].astype(BF16)
                dk[m] = dk[m] + dot(value_ref[rows, col], low)
                dv[m] = dv[m] + dot_nt(key_ref[rows, col], low)
            dq_ref[rows, col] = dq[m]
            dk_ref[rows, col] = dk[m]
            dv_ref[rows, col] = dv[m]


def low_states(state_refs, col, spot_ref):
    kept = [(ref[col, :].astype(F32) * upper(spot_ref, j).astype(F32)).astype(BF16) for j, ref in enumerate(state_refs)]
    return jnp.concatenate(kept, axis=0)


def low_back(back_refs, col, spot_ref):
    kept = [ref[col, :].astype(F32) * (1 - upper(spot_ref, j)).astype(F32) for j, ref in enumerate(back_refs)]
    return functools.reduce(jnp.add, kept).astype(BF16)


def far(spot_ref, top):
    return upper(spot_ref, top) > 0


def base_kernel(span, spot_ref, mixed_ref, weighted_ref, *refs):
    got_refs, out_ref = refs[:-1], refs[-1]
    for i, col in enumerate(head_slices(mixed_ref.shape[1])):
        total = mixed_ref[:, col]
        if got_refs:
            at = i * span * HEAD_DIM
            weighted = weighted_ref[:, at : at + len(got_refs) * HEAD_DIM]
            total = total + dot(weighted, low_states(got_refs, col, spot_ref))
        out_ref[:, col] = total


def early_kernel(tiers, top, spot_ref, dq_ref, dk_ref, dv_ref, key_ref, value_ref, grad_ref, tier_ref, *refs):
    base_ref, weight_ref = refs[:2]
    got_refs, (dq_out, part_ref, dk_low, dv_low) = refs[2:-4], refs[-4:]
    cols = head_slices(dq_ref.shape[1])
    for col in cols:
        total = dq_ref[:, col]
        if got_refs:
            rest = dot_nt(grad_ref[:, col], low_states(got_refs, col, spot_ref))
            for j in range(top):
                scale = tier_ref[:, tiers + j : tiers + j + 1]
                total = total + scale * rest[:, j * HEAD_DIM : (j + 1) * HEAD_DIM]
        dq_out[:, col] = total

    @pl.when(jnp.logical_not(far(spot_ref, top)))
    def _():
        part_ref[...] = dot(base_ref[...].astype(BF16), weight_ref[...])

    @pl.when(far(spot_ref, top))
    def _():
        for col in cols:
            dk, dv = dk_ref[:, col], dv_ref[:, col]
            if got_refs:
                back = low_back(got_refs, col, spot_ref)
                dk = dk + dot(value_ref[:, col], back)
                dv = dv + dot_nt(key_ref[:, col], back)
            dk_low[:, col] = dk.astype(BF16)
            dv_low[:, col] = dv.astype(BF16)


def near_layer_kernel(top, spot_ref, part_ref, base_ref, weight_ref, dq_ref, out_ref, dq_low):
    @pl.when(jnp.logical_not(far(spot_ref, top)))
    def _():
        out_ref[...] = (part_ref[...] + dot(base_ref[...].astype(BF16), weight_ref[...])).astype(BF16)
        dq_low[...] = dq_ref[...].astype(BF16)


def top_columns(weighted_ref, i, span):
    at = (i * span + span - 1) * HEAD_DIM
    return weighted_ref[:, at : at + HEAD_DIM]


def finish_kernel(tiers, spot_ref, dk_ref, dv_ref, key_ref, value_ref, dq_ref, grad_ref, tier_ref, *refs):
    base_ref, weighted_ref, weight_ref, near_layer, near_dq, far_dk, far_dv = refs[:7]
    got_refs = refs[7:-9]
    out_hbm, dq_hbm, dk_hbm, dv_hbm, part_ref, dq_low, dk_low, dv_low, sems = refs[-9:]
    span = len(got_refs)
    top = span - 1
    cols = head_slices(key_ref.shape[1])

    @pl.when(jnp.logical_not(far(spot_ref, top)))
    def _():
        copies = start_copies([(near_layer, out_hbm), (near_dq, dq_hbm)], sems)
        backs = [low_back(got_refs, col, spot_ref) for col in cols]
        for col, back in zip(cols, backs):
            dk_low[:, col] = (dk_ref[:, col] + dot(value_ref[:, col], back)).astype(BF16)
        copies.append(pltpu.make_async_copy(dk_low, dk_hbm, sems.at[2]))
        copies[-1].start()
        for col, back in zip(cols, backs):
            dv_low[:, col] = (dv_ref[:, col] + dot_nt(key_ref[:, col], back)).astype(BF16)
        copies.append(pltpu.make_async_copy(dv_low, dv_hbm, sems.at[3]))
        copies[-1].start()
        for copy in copies:
            copy.wait()

    @pl.when(far(spot_ref, top))
    def _():
        copies = start_copies([(far_dk, dk_hbm), (far_dv, dv_hbm)], sems)
        mixed = []
        for i, col in enumerate(cols):
            total = base_ref[:, col] + dot(top_columns(weighted_ref, i, span), got_refs[top][col, :])
            mixed.append(total.astype(BF16))
        part_ref[...] = dot(jnp.concatenate(mixed, axis=1), weight_ref[...])
        scale = tier_ref[:, tiers + top : tiers + top + 1]
        for col in cols:
            rest = dot_nt(grad_ref[:, col], got_refs[top][col, :])
            dq_low[:, col] = (dq_ref[:, col] + scale * rest).astype(BF16)
        for copy in copies:
            copy.wait()


def far_layer_kernel(span, spot_ref, part_ref, base_ref, weighted_ref, got_ref, weight_ref, dq_ref, *refs):
    out_hbm, dq_hbm, mixed_low, out_low, sems = refs[2:]

    @pl.when(far(spot_ref, span - 1))
    def _():
        copies = start_copies([(dq_ref, dq_hbm)], sems)
        for i, col in enumerate(head_slices(base_ref.shape[1])):
            total = base_ref[:, col] + dot(top_columns(weighted_ref, i, span), got_ref[col, :])
            mixed_low[:, col] = total.astype(BF16)
        chunks = sems.shape[0] - 1
        rows = part_ref.shape[0] // chunks
        for n in range(chunks):
            at = pl.ds(n * rows, rows)
            out_low[at, :] = (part_ref[at, :] + dot(mixed_low[at, :], weight_ref[...])).astype(BF16)
            copies.append(pltpu.make_async_copy(out_low.at[at, :], out_hbm.at[at, :], sems.at[len(copies)]))
            copies[-1].start()
        for copy in copies:
            copy.wait()


def swap_blocks(x, level):
    return lax.ppermute(x, "seq", [(n, n ^ 1 << level) for n in range(lax.axis_size("seq"))])


def add_low(a, b):
    return call(add_kernel, [jax.ShapeDtypeStruct(a.shape, BF16)], [VMEM] * 2, a.size, (a, b), limit=4)[0]


def hbm(*arrays):
    return [pltpu.with_memory_space_constraint(x, pltpu.HBM) for x in arrays]


def on_device(query_in, key_in, value_in, level_mask, out_weight, grad_out):
    blocks = lax.axis_size("seq")
    span = blocks.bit_length() - 1
    if query_in.shape[0] != 1 or lax.axis_size("head") != 2 or blocks != 1 << span:
        raise ValueError("unsupported split")
    query, key, value, mask, grad = (x[0] for x in (query_in, key_in, value_in, level_mask, grad_out))
    length, width = query.shape
    half = grad.shape[1]
    tiers = length.bit_length()
    tile, spans = tiles_of(length)
    siblings = max(1, len(list(sibling_tiles(len(spans)))))
    place = lax.axis_index("head").astype(jnp.int32)[None]
    spot = lax.axis_index("seq").astype(jnp.int32)[None]
    swap = [(0, 1), (1, 0)]
    shape = jax.ShapeDtypeStruct
    dma = pltpu.SemaphoreType.DMA
    matrix = shape((width, HEAD_DIM), BF16)
    low = shape((length, width), BF16)
    high = shape((length, width), F32)
    wide = shape((length, half), BF16)
    low_buffer = pltpu.VMEM((length, width), BF16)
    unit = 2 * length * width * HEAD_DIM
    project = 2 * length * width * half

    grad_other = lax.ppermute(grad, "head", swap)
    state, tier, key, value, weight_own, weight_rest, query, part, weighted = call(
        functools.partial(prep_kernel, tiers, span),
        [matrix, shape((length, mask.shape[1]), F32), low, low]
        + [shape((width, half), BF16)] * 2
        + [low, high, shape((length, span * width), BF16)],
        [SMEM] * 2 + [HBM] * 6,
        project + unit,
        (place, spot, *hbm(mask.T, key, value, grad, out_weight, query)),
        scratch=[pltpu.VMEM(mask.shape[::-1], mask.dtype), pltpu.VMEM((length, half), BF16), dma((7,))],
    )
    grad_mixed, *sends = call(
        functools.partial(reach_kernel, span),
        [low] + [matrix] * span,
        [SMEM] + [VMEM] * 5,
        project + span * unit,
        (spot, grad_other, weight_rest, part, weighted, state),
    )
    weight_other = lax.ppermute(weight_rest, "head", swap)
    weighted_other = lax.ppermute(weighted, "head", swap)
    mixed, probs, blend, inner = call(
        forward_kernel,
        [high, shape((length, width // HEAD_DIM * tile), BF16), shape((length, tile), F32)]
        + [shape((siblings, width, HEAD_DIM), BF16)],
        [VMEM] * 4,
        4 * unit,
        (query, key, value, tier),
    )
    got = []
    for level, total in enumerate(sends):
        for step in range(level):
            total = add_low(total, swap_blocks(total, step))
        got.append(swap_blocks(total, level))
    dq, dk, dv = call(
        backward_kernel, [high] * 3, [VMEM] * 8, 8 * unit, (query, key, value, grad_mixed, tier, probs, blend, inner)
    )
    top = span - 1
    (base,) = call(
        functools.partial(base_kernel, span),
        [high],
        [SMEM] + [VMEM] * (2 + top),
        top * unit,
        (spot, mixed, weighted, *got[:top]),
    )
    base_other = lax.ppermute(base, "head", swap)
    near_dq, part, far_dk, far_dv = call(
        functools.partial(early_kernel, tiers, top),
        [high, shape((length, half), F32), low, low],
        [SMEM] + [VMEM] * (9 + top),
        project + top * unit,
        (spot, dq, dk, dv, key, value, grad_mixed, tier, base, weight_own, *got[:top]),
    )
    near_layer, near_query = call(
        functools.partial(near_layer_kernel, top),
        [wide, low],
        [SMEM] + [VMEM] * 4,
        project,
        (spot, part, base_other, weight_other, near_dq),
    )
    top_other = lax.ppermute(got[top], "head", swap)
    layer_out, grad_query, grad_key, grad_value, part, dq_low = call(
        functools.partial(finish_kernel, tiers),
        [wide, low, low, low, shape((length, half), F32), low],
        [SMEM] + [VMEM] * (14 + span),
        project + 3 * unit,
        (spot, dk, dv, key, value, near_dq, grad_mixed, tier, base, weighted, weight_own)
        + (near_layer, near_query, far_dk, far_dv, *got),
        out_specs=[HBM] * 4 + [VMEM] * 2,
        scratch=[low_buffer] * 2 + [dma((4,))],
    )
    layer_out, grad_query = call(
        functools.partial(far_layer_kernel, span),
        [wide, low],
        [SMEM] + [VMEM] * 6 + [HBM] * 2,
        project + unit,
        (spot, part, base_other, weighted_other, top_other, weight_other, dq_low, layer_out, grad_query),
        out_specs=[HBM] * 2,
        scratch=[low_buffer, pltpu.VMEM((length, half), BF16), dma((5,))],
        aliases={7: 0, 8: 1},
    )
    return tuple(x[None] for x in (layer_out, grad_query, grad_key, grad_value))


def solution(mesh):
    rows = P(("groups", "batch"), "seq", "head")
    return jax.shard_map(
        on_device,
        mesh=mesh,
        in_specs=(rows, rows, rows, P(("groups", "batch"), "seq", None), P("head", None), rows),
        out_specs=(rows,) * 4,
        check_vma=False,
    )
```

```python
import functools

import jax
import jax.numpy as jnp
from jax import lax
from jax.experimental import pallas as pl
from jax.experimental.pallas import tpu as pltpu
from jax.sharding import PartitionSpec as P

HEAD_DIM = 128
TILE = 256
F32 = jnp.float32
BF16 = jnp.bfloat16
VMEM = pl.BlockSpec(memory_space=pltpu.VMEM)
SMEM = pl.BlockSpec(memory_space=pltpu.SMEM)
HBM = pl.BlockSpec(memory_space=pltpu.HBM)


def level_scale(level):
    return 1.0 if level == 0 else 2.0 ** (-(level - 1) / 2.0)


def dot(a, b):
    return lax.dot_general(a, b, (((1,), (0,)), ((), ())), preferred_element_type=F32)


def dot_nt(a, b):
    return lax.dot_general(a, b, (((1,), (1,)), ((), ())), preferred_element_type=F32)


def dot_tn(a, b):
    return lax.dot_general(a, b, (((0,), (0,)), ((), ())), preferred_element_type=F32)


def call(kernel, outs, in_specs, flops, args, out_specs=None, scratch=(), limit=16, aliases=None):
    moved = sum(a.size * a.dtype.itemsize for a in args)
    moved += sum(o.size * o.dtype.itemsize for o in outs)
    return pl.pallas_call(
        kernel,
        out_shape=outs,
        in_specs=in_specs,
        out_specs=out_specs or [VMEM] * len(outs),
        scratch_shapes=list(scratch),
        input_output_aliases=aliases or {},
        compiler_params=pltpu.CompilerParams(vmem_limit_bytes=limit << 20),
        cost_estimate=pl.CostEstimate(flops=flops, bytes_accessed=moved, transcendentals=0),
    )(*args)


def head_slices(width):
    return [slice(i * HEAD_DIM, (i + 1) * HEAD_DIM) for i in range(width // HEAD_DIM)]


def upper(spot_ref, bit):
    return (spot_ref[0] >> bit) & 1


def column(ref, index):
    half = ref.shape[1] // 2
    return ref.at[:, pl.ds(pl.multiple_of(index * half, half), half)]


def start_copies(pairs, sems):
    copies = [pltpu.make_async_copy(src, dst, sems.at[n]) for n, (src, dst) in enumerate(pairs)]
    for copy in copies:
        copy.start()
    return copies


def prep_kernel(tiers, span, place_ref, spot_ref, mask_hbm, key_hbm, value_hbm, grad_hbm, weight_hbm, query_hbm, *refs):
    state_ref, tier_ref, key, value, weight, rest, query, part_ref, weighted_ref, mask, grad, sems = refs
    mine, other = column(weight_hbm, place_ref[0]), column(weight_hbm, 1 - place_ref[0])
    sources = [mask_hbm, query_hbm, key_hbm, value_hbm, mine, grad_hbm, other]
    copies = start_copies(zip(sources, [mask, query, key, value, weight, grad, rest]), sems)
    copies[0].wait()
    levels = mask[...].astype(F32)
    rows = [levels[l : l + 1] * jnp.float32(level_scale(l)) for l in range(levels.shape[0])]
    tier = jnp.transpose(jnp.concatenate(rows, axis=0))
    tier_ref[...] = tier
    copies[1].wait()
    length, width = query.shape
    cols = head_slices(width)
    for j in range(span):
        scale = jnp.broadcast_to(tier[:, tiers + j : tiers + j + 1], (length, HEAD_DIM))
        for col in cols:
            at = j * width + col.start
            weighted_ref[:, at : at + HEAD_DIM] = (scale * query[:, col].astype(F32)).astype(BF16)
    copies[2].wait()
    copies[3].wait()
    for col in cols:
        state_ref[col, :] = dot_tn(key[:, col], value[:, col]).astype(BF16)
    copies[4].wait()
    copies[5].wait()
    part_ref[...] = dot_nt(grad[...], weight[...])
    copies[6].wait()


def reach_kernel(span, spot_ref, grad_ref, weight_ref, part_ref, weighted_ref, state_ref, *outs):
    grad_mixed_ref, send_refs = outs[0], outs[1:]
    grad_mixed = (part_ref[...] + dot_nt(grad_ref[...], weight_ref[...])).astype(BF16)
    grad_mixed_ref[...] = grad_mixed
    width = grad_mixed.shape[1]
    for col in head_slices(width):
        pieces = [weighted_ref[:, j * width + col.start : j * width + col.stop] for j in range(span)]
        reach = dot_tn(grad_mixed[:, col], jnp.concatenate(pieces, axis=1))
        state = state_ref[col, :].astype(F32)
        for j in range(span):
            send = jnp.where(upper(spot_ref, j) > 0, reach[:, j * HEAD_DIM : (j + 1) * HEAD_DIM], state)
            send_refs[j][col, :] = send.astype(BF16)


def add_kernel(a_ref, b_ref, out_ref):
    out_ref[...] = (a_ref[...].astype(F32) + b_ref[...].astype(F32)).astype(BF16)


def tile_blend(tier, tile):
    rows = lax.broadcasted_iota(jnp.int32, (tile, tile), 0)
    cols = lax.broadcasted_iota(jnp.int32, (tile, tile), 1)
    spread = rows ^ cols
    blend = jnp.where(spread == 0, tier[:, 0:1], 0.0)
    for level in range(1, tile.bit_length()):
        here = ((spread >> (level - 1)) == 1) & (cols < rows)
        blend = jnp.where(here, tier[:, level : level + 1], blend)
    return blend


def tiles_of(length):
    tile = min(TILE, length)
    return tile, [slice(i * tile, (i + 1) * tile) for i in range(length // tile)]


def sibling_tiles(count):
    for i in range(count):
        for b in range(count.bit_length() - 1):
            if i >> b & 1:
                first = ((i >> b) ^ 1) << b
                yield i, b, range(first, first + (1 << b))


def forward_kernel(query_ref, key_ref, value_ref, tier_ref, mixed_ref, probs_ref, blend_ref, state_ref):
    length, width = query_ref.shape
    tile, spans = tiles_of(length)
    inner = tile.bit_length()
    for rows in spans:
        blend_ref[rows, :] = tile_blend(tier_ref[rows, :], tile)
    for h, col in enumerate(head_slices(width)):
        mixed = []
        for rows in spans:
            probs = (blend_ref[rows, :] * dot_nt(query_ref[rows, col], key_ref[rows, col])).astype(BF16)
            probs_ref[rows, h * tile : (h + 1) * tile] = probs
            mixed.append(dot(probs, value_ref[rows, col]))
        states = [dot_tn(key_ref[rows, col], value_ref[rows, col]) for rows in spans[:-1]]
        for n, (i, b, members) in enumerate(sibling_tiles(len(spans))):
            total = functools.reduce(jnp.add, [states[m] for m in members]).astype(BF16)
            state_ref[n, col, :] = total
            weight = tier_ref[spans[i], inner + b : inner + b + 1]
            weighted = (weight * query_ref[spans[i], col].astype(F32)).astype(BF16)
            mixed[i] = mixed[i] + dot(weighted, total)
        for rows, value in zip(spans, mixed):
            mixed_ref[rows, col] = value


def backward_kernel(query_ref, key_ref, value_ref, grad_ref, tier_ref, probs_ref, blend_ref, state_ref, *outs):
    dq_ref, dk_ref, dv_ref = outs
    length, width = query_ref.shape
    tile, spans = tiles_of(length)
    inner = tile.bit_length()
    for h, col in enumerate(head_slices(width)):
        dq, dk, dv = [], [], []
        for rows in spans:
            query, key, value, grad = (ref[rows, col] for ref in (query_ref, key_ref, value_ref, grad_ref))
            dscore = (blend_ref[rows, :] * dot_nt(grad, value)).astype(BF16)
            dq.append(dot(dscore, key))
            dk.append(dot_tn(dscore, query))
            dv.append(dot_tn(probs_ref[rows, h * tile : (h + 1) * tile], grad))
        backs = [None] * len(spans)
        for n, (i, b, members) in enumerate(sibling_tiles(len(spans))):
            grad = grad_ref[spans[i], col]
            weight = tier_ref[spans[i], inner + b : inner + b + 1]
            weighted = (weight * query_ref[spans[i], col].astype(F32)).astype(BF16)
            dq[i] = dq[i] + weight * dot_nt(grad, state_ref[n, col, :])
            reach = dot_tn(grad, weighted)
            for m in members:
                backs[m] = reach if backs[m] is None else backs[m] + reach
        for m, rows in enumerate(spans):
            if backs[m] is not None:
                low = backs[m].astype(BF16)
                dk[m] = dk[m] + dot(value_ref[rows, col], low)
                dv[m] = dv[m] + dot_nt(key_ref[rows, col], low)
            dq_ref[rows, col] = dq[m]
            dk_ref[rows, col] = dk[m]
            dv_ref[rows, col] = dv[m]


def head_pairs(width):
    cols = head_slices(width)
    pairs = [cols[i : i + 2] for i in range(0, len(cols), 2)]
    return [(pair, slice(pair[0].start, pair[-1].stop)) for pair in pairs]


def block_diagonal(blocks):
    zero = jnp.zeros_like(blocks[0])
    rows = [jnp.concatenate([x if i == j else zero for j in range(len(blocks))], axis=1) for i, x in enumerate(blocks)]
    return jnp.concatenate(rows, axis=0)


def far(spot_ref, top):
    return upper(spot_ref, top) > 0


def low_state(ref, pair, spot_ref, level):
    keep = upper(spot_ref, level).astype(F32)
    return block_diagonal([(ref[col, :].astype(F32) * keep).astype(BF16) for col in pair])


def low_back(refs, pair, spot_ref):
    blocks = []
    for col in pair:
        kept = [ref[col, :].astype(F32) * (1 - upper(spot_ref, j)).astype(F32) for j, ref in enumerate(refs)]
        blocks.append(functools.reduce(jnp.add, kept).astype(BF16))
    return block_diagonal(blocks)


def base_kernel(spot_ref, mixed_ref, weighted_ref, *refs):
    got_refs, out_ref = refs[:-1], refs[-1]
    width = mixed_ref.shape[1]
    for pair, cols in head_pairs(width):
        total = mixed_ref[:, cols]
        for j, ref in enumerate(got_refs):
            weighted = weighted_ref[:, j * width + cols.start : j * width + cols.stop]
            total = total + dot(weighted, low_state(ref, pair, spot_ref, j))
        out_ref[:, cols] = total


def early_kernel(tiers, top, spot_ref, dq_ref, dk_ref, dv_ref, key_ref, value_ref, grad_ref, tier_ref, *refs):
    base_ref, weight_ref = refs[:2]
    got_refs, (dq_out, part_ref, dk_low, dv_low) = refs[2:-4], refs[-4:]
    pairs = head_pairs(dq_ref.shape[1])
    for pair, cols in pairs:
        total = dq_ref[:, cols]
        for j, ref in enumerate(got_refs):
            rest = dot_nt(grad_ref[:, cols], low_state(ref, pair, spot_ref, j))
            total = total + tier_ref[:, tiers + j : tiers + j + 1] * rest
        dq_out[:, cols] = total

    @pl.when(jnp.logical_not(far(spot_ref, top)))
    def _():
        part_ref[...] = dot(base_ref[...].astype(BF16), weight_ref[...])

    @pl.when(far(spot_ref, top))
    def _():
        for pair, cols in pairs:
            dk, dv = dk_ref[:, cols], dv_ref[:, cols]
            if got_refs:
                back = low_back(got_refs, pair, spot_ref)
                dk = dk + dot(value_ref[:, cols], back)
                dv = dv + dot_nt(key_ref[:, cols], back)
            dk_low[:, cols] = dk.astype(BF16)
            dv_low[:, cols] = dv.astype(BF16)


def near_layer_kernel(top, spot_ref, part_ref, base_ref, weight_ref, dq_ref, out_ref, dq_low):
    @pl.when(jnp.logical_not(far(spot_ref, top)))
    def _():
        out_ref[...] = (part_ref[...] + dot(base_ref[...].astype(BF16), weight_ref[...])).astype(BF16)
        dq_low[...] = dq_ref[...].astype(BF16)


def top_mixed(base_ref, weighted_ref, got_ref):
    width = base_ref.shape[1]
    mixed = []
    for pair, cols in head_pairs(width):
        weighted = weighted_ref[:, pl.ds(weighted_ref.shape[1] - width + cols.start, cols.stop - cols.start)]
        state = block_diagonal([got_ref[col, :] for col in pair])
        mixed.append((base_ref[:, cols] + dot(weighted, state)).astype(BF16))
    return jnp.concatenate(mixed, axis=1)


def finish_kernel(tiers, spot_ref, dk_ref, dv_ref, key_ref, value_ref, dq_ref, grad_ref, tier_ref, *refs):
    base_ref, weighted_ref, weight_ref, near_layer, near_dq, far_dk, far_dv = refs[:7]
    got_refs = refs[7:-9]
    out_hbm, dq_hbm, dk_hbm, dv_hbm, part_ref, dq_low, dk_low, dv_low, sems = refs[-9:]
    top = len(got_refs) - 1
    pairs = head_pairs(key_ref.shape[1])

    @pl.when(jnp.logical_not(far(spot_ref, top)))
    def _():
        copies = start_copies([(near_layer, out_hbm), (near_dq, dq_hbm)], sems)
        backs = [low_back(got_refs, pair, spot_ref) for pair, _ in pairs]
        for (_, cols), back in zip(pairs, backs):
            dk_low[:, cols] = (dk_ref[:, cols] + dot(value_ref[:, cols], back)).astype(BF16)
        copies.append(pltpu.make_async_copy(dk_low, dk_hbm, sems.at[2]))
        copies[-1].start()
        for (_, cols), back in zip(pairs, backs):
            dv_low[:, cols] = (dv_ref[:, cols] + dot_nt(key_ref[:, cols], back)).astype(BF16)
        copies.append(pltpu.make_async_copy(dv_low, dv_hbm, sems.at[3]))
        copies[-1].start()
        for copy in copies:
            copy.wait()

    @pl.when(far(spot_ref, top))
    def _():
        copies = start_copies([(far_dk, dk_hbm), (far_dv, dv_hbm)], sems)
        part_ref[...] = dot(top_mixed(base_ref, weighted_ref, got_refs[top]), weight_ref[...])
        scale = tier_ref[:, tiers + top : tiers + top + 1]
        for pair, cols in pairs:
            rest = dot_nt(grad_ref[:, cols], block_diagonal([got_refs[top][col, :] for col in pair]))
            dq_low[:, cols] = (dq_ref[:, cols] + scale * rest).astype(BF16)
        for copy in copies:
            copy.wait()


def far_layer_kernel(top, spot_ref, part_ref, base_ref, weighted_ref, got_ref, weight_ref, dq_ref, *refs):
    out_hbm, dq_hbm, mixed_low, out_low, sems = refs[2:]

    @pl.when(far(spot_ref, top))
    def _():
        copies = start_copies([(dq_ref, dq_hbm)], sems)
        mixed_low[...] = top_mixed(base_ref, weighted_ref, got_ref)
        chunks = sems.shape[0] - 1
        rows = part_ref.shape[0] // chunks
        for n in range(chunks):
            at = pl.ds(n * rows, rows)
            out_low[at, :] = (part_ref[at, :] + dot(mixed_low[at, :], weight_ref[...])).astype(BF16)
            copies.append(pltpu.make_async_copy(out_low.at[at, :], out_hbm.at[at, :], sems.at[len(copies)]))
            copies[-1].start()
        for copy in copies:
            copy.wait()


def swap_blocks(x, level):
    return lax.ppermute(x, "seq", [(n, n ^ 1 << level) for n in range(lax.axis_size("seq"))])


def add_low(a, b):
    return call(add_kernel, [jax.ShapeDtypeStruct(a.shape, BF16)], [VMEM] * 2, a.size, (a, b), limit=4)[0]


def hbm(*arrays):
    return [pltpu.with_memory_space_constraint(x, pltpu.HBM) for x in arrays]


def on_device(query_in, key_in, value_in, level_mask, out_weight, grad_out):
    blocks = lax.axis_size("seq")
    span = blocks.bit_length() - 1
    if query_in.shape[0] != 1 or lax.axis_size("head") != 2 or blocks != 1 << span:
        raise ValueError("unsupported split")
    query, key, value, mask, grad = (x[0] for x in (query_in, key_in, value_in, level_mask, grad_out))
    length, width = query.shape
    half = grad.shape[1]
    tiers = length.bit_length()
    tile, spans = tiles_of(length)
    siblings = max(1, len(list(sibling_tiles(len(spans)))))
    place = lax.axis_index("head").astype(jnp.int32)[None]
    spot = lax.axis_index("seq").astype(jnp.int32)[None]
    swap = [(0, 1), (1, 0)]
    shape = jax.ShapeDtypeStruct
    dma = pltpu.SemaphoreType.DMA
    matrix = shape((width, HEAD_DIM), BF16)
    low = shape((length, width), BF16)
    high = shape((length, width), F32)
    wide = shape((length, half), BF16)
    low_buffer = pltpu.VMEM((length, width), BF16)
    unit = 2 * length * width * HEAD_DIM
    project = 2 * length * width * half

    grad_other = lax.ppermute(grad, "head", swap)
    state, tier, key, value, weight_own, weight_rest, query, part, weighted = call(
        functools.partial(prep_kernel, tiers, span),
        [matrix, shape((length, mask.shape[1]), F32), low, low]
        + [shape((width, half), BF16)] * 2
        + [low, high, shape((length, span * width), BF16)],
        [SMEM] * 2 + [HBM] * 6,
        project + unit,
        (place, spot, *hbm(mask.T, key, value, grad, out_weight, query)),
        scratch=[pltpu.VMEM(mask.shape[::-1], mask.dtype), pltpu.VMEM((length, half), BF16), dma((7,))],
    )
    grad_mixed, *sends = call(
        functools.partial(reach_kernel, span),
        [low] + [matrix] * span,
        [SMEM] + [VMEM] * 5,
        project + span * unit,
        (spot, grad_other, weight_rest, part, weighted, state),
    )
    weight_other = lax.ppermute(weight_rest, "head", swap)
    weighted_other = lax.ppermute(weighted, "head", swap)
    mixed, probs, blend, inner = call(
        forward_kernel,
        [high, shape((length, width // HEAD_DIM * tile), BF16), shape((length, tile), F32)]
        + [shape((siblings, width, HEAD_DIM), BF16)],
        [VMEM] * 4,
        4 * unit,
        (query, key, value, tier),
    )
    got = []
    for level, total in enumerate(sends):
        for step in range(level):
            total = add_low(total, swap_blocks(total, step))
        got.append(swap_blocks(total, level))
    dq, dk, dv = call(
        backward_kernel, [high] * 3, [VMEM] * 8, 8 * unit, (query, key, value, grad_mixed, tier, probs, blend, inner)
    )
    top = span - 1
    (base,) = call(base_kernel, [high], [SMEM] + [VMEM] * (2 + top), top * unit, (spot, mixed, weighted, *got[:top]))
    base_other = lax.ppermute(base, "head", swap)
    near_dq, part, far_dk, far_dv = call(
        functools.partial(early_kernel, tiers, top),
        [high, shape((length, half), F32), low, low],
        [SMEM] + [VMEM] * (9 + top),
        project + top * unit,
        (spot, dq, dk, dv, key, value, grad_mixed, tier, base, weight_own, *got[:top]),
    )
    near_layer, near_query = call(
        functools.partial(near_layer_kernel, top),
        [wide, low],
        [SMEM] + [VMEM] * 4,
        project,
        (spot, part, base_other, weight_other, near_dq),
    )
    top_other = lax.ppermute(got[top], "head", swap)
    layer_out, grad_query, grad_key, grad_value, part, dq_low = call(
        functools.partial(finish_kernel, tiers),
        [wide, low, low, low, shape((length, half), F32), low],
        [SMEM] + [VMEM] * (14 + span),
        project + 3 * unit,
        (spot, dk, dv, key, value, near_dq, grad_mixed, tier, base, weighted, weight_own)
        + (near_layer, near_query, far_dk, far_dv, *got),
        out_specs=[HBM] * 4 + [VMEM] * 2,
        scratch=[low_buffer] * 2 + [dma((4,))],
    )
    layer_out, grad_query = call(
        functools.partial(far_layer_kernel, top),
        [wide, low],
        [SMEM] + [VMEM] * 6 + [HBM] * 2,
        project + unit,
        (spot, part, base_other, weighted_other, top_other, weight_other, dq_low, layer_out, grad_query),
        out_specs=[HBM] * 2,
        scratch=[low_buffer, pltpu.VMEM((length, half), BF16), dma((5,))],
        aliases={7: 0, 8: 1},
    )
    return tuple(x[None] for x in (layer_out, grad_query, grad_key, grad_value))


def solution(mesh):
    rows = P(("groups", "batch"), "seq", "head")
    return jax.shard_map(
        on_device,
        mesh=mesh,
        in_specs=(rows, rows, rows, P(("groups", "batch"), "seq", None), P("head", None), rows),
        out_specs=(rows,) * 4,
        check_vma=False,
    )
```

```python
import functools

import jax
import jax.numpy as jnp
from jax import lax
from jax.experimental import pallas as pl
from jax.experimental.pallas import tpu as pltpu
from jax.sharding import PartitionSpec as P

HEAD_DIM = 128
TILE = 256
F32 = jnp.float32
BF16 = jnp.bfloat16
VMEM = pl.BlockSpec(memory_space=pltpu.VMEM)
SMEM = pl.BlockSpec(memory_space=pltpu.SMEM)
HBM = pl.BlockSpec(memory_space=pltpu.HBM)


def level_scale(level):
    return 1.0 if level == 0 else 2.0 ** (-(level - 1) / 2.0)


def dot(a, b):
    return lax.dot_general(a, b, (((1,), (0,)), ((), ())), preferred_element_type=F32)


def dot_nt(a, b):
    return lax.dot_general(a, b, (((1,), (1,)), ((), ())), preferred_element_type=F32)


def dot_tn(a, b):
    return lax.dot_general(a, b, (((0,), (0,)), ((), ())), preferred_element_type=F32)


def call(kernel, outs, in_specs, flops, args, out_specs=None, scratch=(), limit=16, aliases=None):
    moved = sum(a.size * a.dtype.itemsize for a in args)
    moved += sum(o.size * o.dtype.itemsize for o in outs)
    return pl.pallas_call(
        kernel,
        out_shape=outs,
        in_specs=in_specs,
        out_specs=out_specs or [VMEM] * len(outs),
        scratch_shapes=list(scratch),
        input_output_aliases=aliases or {},
        compiler_params=pltpu.CompilerParams(vmem_limit_bytes=limit << 20),
        cost_estimate=pl.CostEstimate(flops=flops, bytes_accessed=moved, transcendentals=0),
    )(*args)


def head_slices(width):
    return [slice(i * HEAD_DIM, (i + 1) * HEAD_DIM) for i in range(width // HEAD_DIM)]


def upper(spot_ref, bit):
    return (spot_ref[0] >> bit) & 1


def column(ref, index):
    half = ref.shape[1] // 2
    return ref.at[:, pl.ds(pl.multiple_of(index * half, half), half)]


def start_copies(pairs, sems):
    copies = [pltpu.make_async_copy(src, dst, sems.at[n]) for n, (src, dst) in enumerate(pairs)]
    for copy in copies:
        copy.start()
    return copies


def prep_kernel(tiers, span, place_ref, spot_ref, mask_hbm, key_hbm, value_hbm, grad_hbm, weight_hbm, query_hbm, *refs):
    state_ref, tier_ref, key, value, weight, rest, query, part_ref, weighted_ref, mask, grad, sems = refs
    mine, other = column(weight_hbm, place_ref[0]), column(weight_hbm, 1 - place_ref[0])
    sources = [mask_hbm, query_hbm, key_hbm, value_hbm, mine, grad_hbm, other]
    copies = start_copies(zip(sources, [mask, query, key, value, weight, grad, rest]), sems)
    copies[0].wait()
    levels = mask[...].astype(F32)
    rows = [levels[l : l + 1] * jnp.float32(level_scale(l)) for l in range(levels.shape[0])]
    tier = jnp.transpose(jnp.concatenate(rows, axis=0))
    tier_ref[...] = tier
    copies[1].wait()
    length, width = query.shape
    cols = head_slices(width)
    for j in range(span):
        scale = jnp.broadcast_to(tier[:, tiers + j : tiers + j + 1], (length, HEAD_DIM))
        for col in cols:
            at = j * width + col.start
            weighted_ref[:, at : at + HEAD_DIM] = (scale * query[:, col].astype(F32)).astype(BF16)
    copies[2].wait()
    copies[3].wait()
    for col in cols:
        state_ref[col, :] = dot_tn(key[:, col], value[:, col]).astype(BF16)
    copies[4].wait()
    copies[5].wait()
    part_ref[...] = dot_nt(grad[...], weight[...])
    copies[6].wait()


def reach_kernel(span, spot_ref, grad_ref, weight_ref, part_ref, weighted_ref, state_ref, *outs):
    grad_mixed_ref, send_refs = outs[0], outs[1:]
    grad_mixed = (part_ref[...] + dot_nt(grad_ref[...], weight_ref[...])).astype(BF16)
    grad_mixed_ref[...] = grad_mixed
    width = grad_mixed.shape[1]
    for col in head_slices(width):
        pieces = [weighted_ref[:, j * width + col.start : j * width + col.stop] for j in range(span)]
        reach = dot_tn(grad_mixed[:, col], jnp.concatenate(pieces, axis=1))
        state = state_ref[col, :].astype(F32)
        for j in range(span):
            send = jnp.where(upper(spot_ref, j) > 0, reach[:, j * HEAD_DIM : (j + 1) * HEAD_DIM], state)
            send_refs[j][col, :] = send.astype(BF16)


def half_kernel(spot_ref, sent_ref, keep_ref, give_ref):
    half = keep_ref.shape[0]
    odd = upper(spot_ref, 0) > 0
    first, second = sent_ref[:half, :], sent_ref[half:, :]
    keep_ref[...] = jnp.where(odd, second, first)
    give_ref[...] = jnp.where(odd, first, second)


def join_kernel(spot_ref, same_ref, cross_ref, out_ref):
    half = same_ref.shape[0]
    odd = upper(spot_ref, 0) > 0
    out_ref[:half, :] = jnp.where(odd, cross_ref[...], same_ref[...])
    out_ref[half:, :] = jnp.where(odd, same_ref[...], cross_ref[...])


def add_kernel(a_ref, b_ref, out_ref):
    out_ref[...] = (a_ref[...].astype(F32) + b_ref[...].astype(F32)).astype(BF16)


def tile_blend(tier, tile):
    rows = lax.broadcasted_iota(jnp.int32, (tile, tile), 0)
    cols = lax.broadcasted_iota(jnp.int32, (tile, tile), 1)
    spread = rows ^ cols
    blend = jnp.where(spread == 0, tier[:, 0:1], 0.0)
    for level in range(1, tile.bit_length()):
        here = ((spread >> (level - 1)) == 1) & (cols < rows)
        blend = jnp.where(here, tier[:, level : level + 1], blend)
    return blend


def tiles_of(length):
    tile = min(TILE, length)
    return tile, [slice(i * tile, (i + 1) * tile) for i in range(length // tile)]


def sibling_tiles(count):
    for i in range(count):
        for b in range(count.bit_length() - 1):
            if i >> b & 1:
                first = ((i >> b) ^ 1) << b
                yield i, b, range(first, first + (1 << b))


def forward_kernel(query_ref, key_ref, value_ref, tier_ref, mixed_ref, probs_ref, blend_ref, state_ref):
    length, width = query_ref.shape
    tile, spans = tiles_of(length)
    inner = tile.bit_length()
    for rows in spans:
        blend_ref[rows, :] = tile_blend(tier_ref[rows, :], tile)
    for h, col in enumerate(head_slices(width)):
        mixed = []
        for rows in spans:
            probs = (blend_ref[rows, :] * dot_nt(query_ref[rows, col], key_ref[rows, col])).astype(BF16)
            probs_ref[rows, h * tile : (h + 1) * tile] = probs
            mixed.append(dot(probs, value_ref[rows, col]))
        states = [dot_tn(key_ref[rows, col], value_ref[rows, col]) for rows in spans[:-1]]
        for n, (i, b, members) in enumerate(sibling_tiles(len(spans))):
            total = functools.reduce(jnp.add, [states[m] for m in members]).astype(BF16)
            state_ref[n, col, :] = total
            weight = tier_ref[spans[i], inner + b : inner + b + 1]
            weighted = (weight * query_ref[spans[i], col].astype(F32)).astype(BF16)
            mixed[i] = mixed[i] + dot(weighted, total)
        for rows, value in zip(spans, mixed):
            mixed_ref[rows, col] = value


def backward_kernel(query_ref, key_ref, value_ref, grad_ref, tier_ref, probs_ref, blend_ref, state_ref, *outs):
    dq_ref, dk_ref, dv_ref = outs
    length, width = query_ref.shape
    tile, spans = tiles_of(length)
    inner = tile.bit_length()
    for h, col in enumerate(head_slices(width)):
        dq, dk, dv = [], [], []
        for rows in spans:
            query, key, value, grad = (ref[rows, col] for ref in (query_ref, key_ref, value_ref, grad_ref))
            dscore = (blend_ref[rows, :] * dot_nt(grad, value)).astype(BF16)
            dq.append(dot(dscore, key))
            dk.append(dot_tn(dscore, query))
            dv.append(dot_tn(probs_ref[rows, h * tile : (h + 1) * tile], grad))
        backs = [None] * len(spans)
        for n, (i, b, members) in enumerate(sibling_tiles(len(spans))):
            grad = grad_ref[spans[i], col]
            weight = tier_ref[spans[i], inner + b : inner + b + 1]
            weighted = (weight * query_ref[spans[i], col].astype(F32)).astype(BF16)
            dq[i] = dq[i] + weight * dot_nt(grad, state_ref[n, col, :])
            reach = dot_tn(grad, weighted)
            for m in members:
                backs[m] = reach if backs[m] is None else backs[m] + reach
        for m, rows in enumerate(spans):
            if backs[m] is not None:
                low = backs[m].astype(BF16)
                dk[m] = dk[m] + dot(value_ref[rows, col], low)
                dv[m] = dv[m] + dot_nt(key_ref[rows, col], low)
            dq_ref[rows, col] = dq[m]
            dk_ref[rows, col] = dk[m]
            dv_ref[rows, col] = dv[m]


def head_pairs(width):
    cols = head_slices(width)
    pairs = [cols[i : i + 2] for i in range(0, len(cols), 2)]
    return [(pair, slice(pair[0].start, pair[-1].stop)) for pair in pairs]


def block_diagonal(blocks):
    zero = jnp.zeros_like(blocks[0])
    rows = [jnp.concatenate([x if i == j else zero for j in range(len(blocks))], axis=1) for i, x in enumerate(blocks)]
    return jnp.concatenate(rows, axis=0)


def far(spot_ref, top):
    return upper(spot_ref, top) > 0


def low_state(ref, pair, spot_ref, level):
    keep = upper(spot_ref, level).astype(F32)
    return block_diagonal([(ref[col, :].astype(F32) * keep).astype(BF16) for col in pair])


def low_back(refs, pair, spot_ref):
    blocks = []
    for col in pair:
        kept = [ref[col, :].astype(F32) * (1 - upper(spot_ref, j)).astype(F32) for j, ref in enumerate(refs)]
        blocks.append(functools.reduce(jnp.add, kept).astype(BF16))
    return block_diagonal(blocks)


def base_kernel(spot_ref, mixed_ref, weighted_ref, *refs):
    got_refs, out_ref = refs[:-1], refs[-1]
    width = mixed_ref.shape[1]
    for pair, cols in head_pairs(width):
        total = mixed_ref[:, cols]
        for j, ref in enumerate(got_refs):
            weighted = weighted_ref[:, j * width + cols.start : j * width + cols.stop]
            total = total + dot(weighted, low_state(ref, pair, spot_ref, j))
        out_ref[:, cols] = total


def early_kernel(tiers, top, spot_ref, dq_ref, dk_ref, dv_ref, key_ref, value_ref, grad_ref, tier_ref, *refs):
    base_ref, weight_ref = refs[:2]
    got_refs, (dq_out, part_ref, dk_low, dv_low) = refs[2:-4], refs[-4:]
    pairs = head_pairs(dq_ref.shape[1])
    for pair, cols in pairs:
        total = dq_ref[:, cols]
        for j, ref in enumerate(got_refs):
            rest = dot_nt(grad_ref[:, cols], low_state(ref, pair, spot_ref, j))
            total = total + tier_ref[:, tiers + j : tiers + j + 1] * rest
        dq_out[:, cols] = total

    @pl.when(jnp.logical_not(far(spot_ref, top)))
    def _():
        part_ref[...] = dot(base_ref[...].astype(BF16), weight_ref[...])

    @pl.when(far(spot_ref, top))
    def _():
        for pair, cols in pairs:
            dk, dv = dk_ref[:, cols], dv_ref[:, cols]
            if got_refs:
                back = low_back(got_refs, pair, spot_ref)
                dk = dk + dot(value_ref[:, cols], back)
                dv = dv + dot_nt(key_ref[:, cols], back)
            dk_low[:, cols] = dk.astype(BF16)
            dv_low[:, cols] = dv.astype(BF16)


def near_layer_kernel(top, spot_ref, part_ref, base_ref, weight_ref, dq_ref, out_ref, dq_low):
    @pl.when(jnp.logical_not(far(spot_ref, top)))
    def _():
        out_ref[...] = (part_ref[...] + dot(base_ref[...].astype(BF16), weight_ref[...])).astype(BF16)
        dq_low[...] = dq_ref[...].astype(BF16)


def top_mixed(base_ref, weighted_ref, got_ref):
    width = base_ref.shape[1]
    mixed = []
    for pair, cols in head_pairs(width):
        weighted = weighted_ref[:, pl.ds(weighted_ref.shape[1] - width + cols.start, cols.stop - cols.start)]
        state = block_diagonal([got_ref[col, :] for col in pair])
        mixed.append((base_ref[:, cols] + dot(weighted, state)).astype(BF16))
    return jnp.concatenate(mixed, axis=1)


def finish_kernel(tiers, spot_ref, dk_ref, dv_ref, key_ref, value_ref, dq_ref, grad_ref, tier_ref, *refs):
    base_ref, weighted_ref, weight_ref, near_layer, near_dq, far_dk, far_dv = refs[:7]
    got_refs = refs[7:-9]
    out_hbm, dq_hbm, dk_hbm, dv_hbm, part_ref, dq_low, dk_low, dv_low, sems = refs[-9:]
    top = len(got_refs) - 1
    pairs = head_pairs(key_ref.shape[1])

    @pl.when(jnp.logical_not(far(spot_ref, top)))
    def _():
        copies = start_copies([(near_layer, out_hbm), (near_dq, dq_hbm)], sems)
        backs = [low_back(got_refs, pair, spot_ref) for pair, _ in pairs]
        for (_, cols), back in zip(pairs, backs):
            dk_low[:, cols] = (dk_ref[:, cols] + dot(value_ref[:, cols], back)).astype(BF16)
        copies.append(pltpu.make_async_copy(dk_low, dk_hbm, sems.at[2]))
        copies[-1].start()
        for (_, cols), back in zip(pairs, backs):
            dv_low[:, cols] = (dv_ref[:, cols] + dot_nt(key_ref[:, cols], back)).astype(BF16)
        copies.append(pltpu.make_async_copy(dv_low, dv_hbm, sems.at[3]))
        copies[-1].start()
        for copy in copies:
            copy.wait()

    @pl.when(far(spot_ref, top))
    def _():
        copies = start_copies([(far_dk, dk_hbm), (far_dv, dv_hbm)], sems)
        part_ref[...] = dot(top_mixed(base_ref, weighted_ref, got_refs[top]), weight_ref[...])
        scale = tier_ref[:, tiers + top : tiers + top + 1]
        for pair, cols in pairs:
            rest = dot_nt(grad_ref[:, cols], block_diagonal([got_refs[top][col, :] for col in pair]))
            dq_low[:, cols] = (dq_ref[:, cols] + scale * rest).astype(BF16)
        for copy in copies:
            copy.wait()


def far_layer_kernel(top, spot_ref, part_ref, base_ref, weighted_ref, got_ref, weight_ref, dq_ref, *refs):
    out_hbm, dq_hbm, mixed_low, out_low, sems = refs[2:]

    @pl.when(far(spot_ref, top))
    def _():
        copies = start_copies([(dq_ref, dq_hbm)], sems)
        mixed_low[...] = top_mixed(base_ref, weighted_ref, got_ref)
        chunks = sems.shape[0] - 1
        rows = part_ref.shape[0] // chunks
        for n in range(chunks):
            at = pl.ds(n * rows, rows)
            out_low[at, :] = (part_ref[at, :] + dot(mixed_low[at, :], weight_ref[...])).astype(BF16)
            copies.append(pltpu.make_async_copy(out_low.at[at, :], out_hbm.at[at, :], sems.at[len(copies)]))
            copies[-1].start()
        for copy in copies:
            copy.wait()


def swap_blocks(x, level):
    return lax.ppermute(x, "seq", [(n, n ^ 1 << level) for n in range(lax.axis_size("seq"))])


def add_low(a, b):
    return call(add_kernel, [jax.ShapeDtypeStruct(a.shape, BF16)], [VMEM] * 2, a.size, (a, b), limit=4)[0]


def exchange_halves(spot, sent):
    half = jax.ShapeDtypeStruct((sent.shape[0] // 2, HEAD_DIM), BF16)
    keep, give = call(half_kernel, [half] * 2, [SMEM, VMEM], sent.size, (spot, sent), limit=4)
    total = add_low(keep, swap_blocks(give, 0))
    same = swap_blocks(total, 1)
    cross = lax.ppermute(total, "seq", [(n, n ^ 3) for n in range(lax.axis_size("seq"))])
    whole = jax.ShapeDtypeStruct(sent.shape, BF16)
    return call(join_kernel, [whole], [SMEM] + [VMEM] * 2, sent.size, (spot, same, cross), limit=4)[0]


def hbm(*arrays):
    return [pltpu.with_memory_space_constraint(x, pltpu.HBM) for x in arrays]


def on_device(query_in, key_in, value_in, level_mask, out_weight, grad_out):
    blocks = lax.axis_size("seq")
    span = blocks.bit_length() - 1
    if query_in.shape[0] != 1 or lax.axis_size("head") != 2 or blocks != 1 << span:
        raise ValueError("unsupported split")
    query, key, value, mask, grad = (x[0] for x in (query_in, key_in, value_in, level_mask, grad_out))
    length, width = query.shape
    half = grad.shape[1]
    tiers = length.bit_length()
    tile, spans = tiles_of(length)
    siblings = max(1, len(list(sibling_tiles(len(spans)))))
    place = lax.axis_index("head").astype(jnp.int32)[None]
    spot = lax.axis_index("seq").astype(jnp.int32)[None]
    swap = [(0, 1), (1, 0)]
    shape = jax.ShapeDtypeStruct
    dma = pltpu.SemaphoreType.DMA
    matrix = shape((width, HEAD_DIM), BF16)
    low = shape((length, width), BF16)
    high = shape((length, width), F32)
    wide = shape((length, half), BF16)
    low_buffer = pltpu.VMEM((length, width), BF16)
    unit = 2 * length * width * HEAD_DIM
    project = 2 * length * width * half

    grad_other = lax.ppermute(grad, "head", swap)
    state, tier, key, value, weight_own, weight_rest, query, part, weighted = call(
        functools.partial(prep_kernel, tiers, span),
        [matrix, shape((length, mask.shape[1]), F32), low, low]
        + [shape((width, half), BF16)] * 2
        + [low, high, shape((length, span * width), BF16)],
        [SMEM] * 2 + [HBM] * 6,
        project + unit,
        (place, spot, *hbm(mask.T, key, value, grad, out_weight, query)),
        scratch=[pltpu.VMEM(mask.shape[::-1], mask.dtype), pltpu.VMEM((length, half), BF16), dma((7,))],
    )
    grad_mixed, *sends = call(
        functools.partial(reach_kernel, span),
        [low] + [matrix] * span,
        [SMEM] + [VMEM] * 5,
        project + span * unit,
        (spot, grad_other, weight_rest, part, weighted, state),
    )
    weight_other = lax.ppermute(weight_rest, "head", swap)
    weighted_other = lax.ppermute(weighted, "head", swap)
    mixed, probs, blend, inner = call(
        forward_kernel,
        [high, shape((length, width // HEAD_DIM * tile), BF16), shape((length, tile), F32)]
        + [shape((siblings, width, HEAD_DIM), BF16)],
        [VMEM] * 4,
        4 * unit,
        (query, key, value, tier),
    )
    got = []
    for level, total in enumerate(sends):
        if span == 2 and level == 1:
            got.append(exchange_halves(spot, total))
            continue
        for step in range(level):
            total = add_low(total, swap_blocks(total, step))
        got.append(swap_blocks(total, level))
    dq, dk, dv = call(
        backward_kernel, [high] * 3, [VMEM] * 8, 8 * unit, (query, key, value, grad_mixed, tier, probs, blend, inner)
    )
    top = span - 1
    (base,) = call(base_kernel, [high], [SMEM] + [VMEM] * (2 + top), top * unit, (spot, mixed, weighted, *got[:top]))
    base_other = lax.ppermute(base, "head", swap)
    near_dq, part, far_dk, far_dv = call(
        functools.partial(early_kernel, tiers, top),
        [high, shape((length, half), F32), low, low],
        [SMEM] + [VMEM] * (9 + top),
        project + top * unit,
        (spot, dq, dk, dv, key, value, grad_mixed, tier, base, weight_own, *got[:top]),
    )
    near_layer, near_query = call(
        functools.partial(near_layer_kernel, top),
        [wide, low],
        [SMEM] + [VMEM] * 4,
        project,
        (spot, part, base_other, weight_other, near_dq),
    )
    top_other = lax.ppermute(got[top], "head", swap)
    layer_out, grad_query, grad_key, grad_value, part, dq_low = call(
        functools.partial(finish_kernel, tiers),
        [wide, low, low, low, shape((length, half), F32), low],
        [SMEM] + [VMEM] * (14 + span),
        project + 3 * unit,
        (spot, dk, dv, key, value, near_dq, grad_mixed, tier, base, weighted, weight_own)
        + (near_layer, near_query, far_dk, far_dv, *got),
        out_specs=[HBM] * 4 + [VMEM] * 2,
        scratch=[low_buffer] * 2 + [dma((4,))],
    )
    layer_out, grad_query = call(
        functools.partial(far_layer_kernel, top),
        [wide, low],
        [SMEM] + [VMEM] * 6 + [HBM] * 2,
        project + unit,
        (spot, part, base_other, weighted_other, top_other, weight_other, dq_low, layer_out, grad_query),
        out_specs=[HBM] * 2,
        scratch=[low_buffer, pltpu.VMEM((length, half), BF16), dma((5,))],
        aliases={7: 0, 8: 1},
    )
    return tuple(x[None] for x in (layer_out, grad_query, grad_key, grad_value))


def solution(mesh):
    rows = P(("groups", "batch"), "seq", "head")
    return jax.shard_map(
        on_device,
        mesh=mesh,
        in_specs=(rows, rows, rows, P(("groups", "batch"), "seq", None), P("head", None), rows),
        out_specs=(rows,) * 4,
        check_vma=False,
    )
```
